128 devices in a mesh: emb: 16 (over x, z), dp: 8 (over y, core).
Axes of the slice: x: 4, y: 4, z: 4, core: 2. Of those that a mesh axis runs over, the one named last changes fastest.
Arguments:
- user_table: bfloat16 [32768, 512], P('emb'), may hold values from -6 to 6
- item_table: bfloat16 [32768, 512], P('emb'), may hold values from -6 to 6
- user_owner: int32 [262144, 1], P(('emb', 'dp')), may hold values from 0 to 15; in each aligned block of 2048 rows (0 to 2047, 2048 to 4095, ...) at most 192 rows name the same one
- user_row: int32 [262144], P(('emb', 'dp')), may hold values from 0 to 2047
- item_owner: int32 [262144, 1], P(('emb', 'dp')), may hold values from 0 to 15; in each aligned block of 2048 rows (0 to 2047, 2048 to 4095, ...) at most 192 rows name the same one
- item_row: int32 [262144], P(('emb', 'dp')), may hold values from 0 to 2047
- labels: int32 [262144], P(('emb', 'dp')), may hold values 0 or 1
- w1_user: bfloat16 [256, 512], replicated, may hold values from -0.25 to 0.25
- w1_item: bfloat16 [256, 512], replicated, may hold values from -0.25 to 0.25
- w2_weight: bfloat16 [512, 512], replicated, may hold values from -0.25 to 0.25
- w3_weight: bfloat16 [512, 512], replicated, may hold values from -0.25 to 0.25
- w_out: float32 [768], replicated, may hold values from -0.5 to 0.5
Outputs:
- user_grad: float32 [8, 32768, 512], P('dp', 'emb')
- item_grad: float32 [8, 32768, 512], P('dp', 'emb')
- grad_w1_user: float32 [256, 512], replicated
- grad_w1_item: float32 [256, 512], replicated
- grad_w2: float32 [512, 512], replicated
- grad_w3: float32 [512, 512], replicated
- grad_out: float32 [768], replicated
The draws below stay inside these ranges and needn't reach their ends.
Inputs may be any that keep to these rules, and one draw needn't show every extreme that they name: `user_owner`: of the pairs of one device, at most 192 have their user with the same index of emb, and exactly that many in some device. `item_owner`: of the pairs of one device, at most 192 have their item with the same index of emb, and exactly that many in some device.
All inputs are finite; a program needn't handle non-finite values. No bound on the sum of `labels` on one device may be relied on, other than what follows from the above.
Results may differ from the reference program's by a relative error of at most 0.019.
Values may be sent and summed in bfloat16 or wider, within the bound.
No kernel may reach another device: no remote copies, remote signals or barrier semaphores. Data moves between devices by JAX's collectives and lax.ppermute only.
A program may use at most 128 MiB of HBM per device.

```python
import math
import jax
import jax.numpy as jnp
import numpy as np

D_GMF = 256
D_MLP = 256
HID = 512
USER_ROWS = 2048
ITEM_ROWS = 2048
PAIRS_DEV = 2048
CAP = 192
USERS = 32768
ITEMS = 32768
TOTAL_PAIRS = 262144
N_EMB = 16
N_DP = 8


def set_ends(drawn, rng, low, top_value):
    longest = drawn.shape.index(max(drawn.shape))
    spots = []
    for shift in (0, 1):
        where = [jax.random.randint(jax.random.fold_in(rng, axis), (), 0, length) for axis, length in enumerate(drawn.shape)]
        where[longest] = (where[longest] + shift) % drawn.shape[longest]
        spots.append(tuple(where))
    return drawn.at[spots[0]].set(low).at[spots[1]].set(top_value)


def block_scale(rng, extent, split, smallest, largest):
    factor_of = 1.0
    for dim, blocks in split:
        steps = jax.random.uniform(jax.random.fold_in(jax.random.fold_in(rng, 6), dim), (blocks,), jnp.float32, smallest / len(split), largest / len(split))
        factor_of = factor_of * jnp.repeat(jnp.exp(steps), extent[dim] // blocks).reshape((-1,) + (1,) * (len(extent) - 1 - dim))
    return factor_of


def cumulative_ranks(amount, lean):
    loads = [(1 << 20) // math.isqrt(grade ** lean) + 1 for grade in range(1, amount + 1)]
    scale = 1 + sum(loads) // (1 << 30)
    return np.cumsum(np.array([max(1, weight // scale) for weight in loads]))


def ranked_ids(key, extent, number_of, lean):
    grid = cumulative_ranks(number_of, lean)
    lot = jax.random.randint(jax.random.fold_in(key, 1), extent, 0, int(grid[number_of - 1]))
    grade = jnp.searchsorted(jnp.asarray(grid, jnp.int32), lot, side="right")
    return jax.random.permutation(jax.random.fold_in(key, 2), number_of)[grade].astype(jnp.int32)


def assign_block(key, own, number, rows, count, top, most, lean):
    sequence = jax.random.permutation(key, count)
    packed, common = load_shares(count, rows * top, most, lean, True), load_shares(count, rows * top, most, lean, False)
    places = jnp.arange(count)

    def named(lengths, turn):
        used = int((lengths > 0).sum())
        fixed = max(1, used // 4)
        shifted = fixed + (places - fixed + turn * (used - fixed)) % max(1, count - fixed)
        return jnp.zeros((count,), jnp.int32).at[sequence[jnp.where(places < fixed, places, shifted)]].set(jnp.asarray(lengths, jnp.int32))

    lengths = jnp.where(number % 4 == 0, named(packed, number // 4), named(common, number - number // 4 - 1))
    mixed = jax.random.permutation(jax.random.fold_in(own, 3), count)
    donor, sink = mixed[0:count // 2 * 2:2], mixed[1:count // 2 * 2:2]
    room = jnp.minimum(lengths[donor] - 1, most - lengths[sink]) // 2
    room = jnp.where((donor == sequence[0]) | (sink == sequence[0]) | (lengths[sink] == 0), 0, jnp.maximum(room, 0))
    shifted = jax.random.randint(jax.random.fold_in(own, 4), (count // 2,), 0, 1 << 20) % (room + 1)
    lengths = lengths.at[donor].add(-shifted).at[sink].add(shifted)
    items = jnp.searchsorted(jnp.cumsum(lengths), jnp.arange(rows * top), side="right").astype(jnp.int32)
    table = items.reshape(top, rows).T
    table = table[jax.random.permutation(jax.random.fold_in(own, 1), rows)]
    turn = jax.random.randint(jax.random.fold_in(own, 2), (rows, 1), 0, top)
    return jnp.take_along_axis(table, (jnp.arange(top)[None, :] + turn) % top, axis=1)


def load_shares(number_of, total, reach, lean, full):
    loads = [(1 << 20) // math.isqrt(grade ** lean) + 1 for grade in range(1, number_of + 1)]
    largest = reach if full else min(reach, max(-(-total // number_of), total * loads[0] // sum(loads)))
    least = 1 if total - largest >= number_of - 1 else 0
    holding, rest = [largest] + [least] * (number_of - 1), total - largest - least * (number_of - 1)
    while rest > 0:
        free = [i for i in range(1, number_of) if holding[i] < largest] or [i for i in range(1, number_of) if holding[i] < reach]
        mass, remaining = sum([loads[i] for i in free]), rest
        for i in free:
            extra = min(reach - holding[i], max(1, remaining * loads[i] // mass), rest)
            holding[i] = holding[i] + extra
            rest = rest - extra
    return np.array(holding)


def bell_draw(key, dims, scale, most, pieces=(), kind=jnp.bfloat16):
    level = block_scale(key, dims, pieces, -0.22, 0.18) if pieces else 1.0
    values = jax.random.normal(key, dims, jnp.float32) * scale * level
    return jnp.minimum(jnp.maximum(values, -most), most).astype(kind)


def setup_inputs(seed: int = 0) -> dict:
    seeds = jax.random.split(jax.random.key(seed), 13)
    user_table = bell_draw(seeds[0], (USERS, D_GMF + D_MLP), 1.0, 6.0, ((0, 16),))
    item_table = bell_draw(seeds[1], (ITEMS, D_GMF + D_MLP), 1.0, 6.0, ((0, 16),))
    user_owner_keys = jax.random.split(jax.random.fold_in(seeds[2], 1), TOTAL_PAIRS // PAIRS_DEV)
    user_owner_turns = jax.random.permutation(jax.random.fold_in(seeds[2], 3), TOTAL_PAIRS // PAIRS_DEV)
    user_owner = jax.vmap(lambda own, number: assign_block(jax.random.fold_in(seeds[2], 2), own, number, PAIRS_DEV, N_EMB, 1, CAP, 2))(user_owner_keys, user_owner_turns).reshape((TOTAL_PAIRS, 1))
    user_row = set_ends(ranked_ids(seeds[3], (TOTAL_PAIRS,), USER_ROWS, 2), jax.random.fold_in(seeds[3], 3), 0, USER_ROWS - 1).astype(jnp.int32)
    item_owner_keys = jax.random.split(jax.random.fold_in(seeds[4], 1), TOTAL_PAIRS // PAIRS_DEV)
    item_owner_turns = jax.random.permutation(jax.random.fold_in(seeds[4], 3), TOTAL_PAIRS // PAIRS_DEV)
    item_owner = jax.vmap(lambda own, number: assign_block(jax.random.fold_in(seeds[4], 2), own, number, PAIRS_DEV, N_EMB, 1, CAP, 2))(item_owner_keys, item_owner_turns).reshape((TOTAL_PAIRS, 1))
    item_row = set_ends(ranked_ids(seeds[5], (TOTAL_PAIRS,), ITEM_ROWS, 2), jax.random.fold_in(seeds[5], 3), 0, ITEM_ROWS - 1).astype(jnp.int32)
    labels = set_ends((jax.random.randint(seeds[6], (TOTAL_PAIRS,), 0, 2) < 1).astype(jnp.int32), jax.random.fold_in(seeds[6], 1), 0, 1)
    w1_user = bell_draw(seeds[7], (D_MLP, HID), (D_MLP + D_MLP) ** -0.5, 0.25)
    w1_item = bell_draw(seeds[8], (D_MLP, HID), (D_MLP + D_MLP) ** -0.5, 0.25)
    w2_weight = bell_draw(seeds[9], (HID, HID), HID ** -0.5, 0.25)
    w3_weight = bell_draw(seeds[10], (HID, HID), HID ** -0.5, 0.25)
    w_out = bell_draw(seeds[11], (D_GMF + HID,), 128 ** -0.5, 0.5, (), jnp.float32)
    return dict(user_table=user_table, item_table=item_table, user_owner=user_owner, user_row=user_row, item_owner=item_owner, item_row=item_row, labels=labels, w1_user=w1_user, w1_item=w1_item, w2_weight=w2_weight, w3_weight=w3_weight, w_out=w_out)


def silu_slope(pre):
    sig = jax.nn.sigmoid(pre)
    return sig * (1.0 + pre * (1.0 - sig))


def reference(user_table, item_table, user_owner, user_row, item_owner, item_row, labels, w1_user, w1_item, w2_weight, w3_weight, w_out):
    gmf_width = D_GMF
    user_index = (user_owner[:, 0] * USER_ROWS + user_row).astype(jnp.int32)
    item_index = (item_owner[:, 0] * ITEM_ROWS + item_row).astype(jnp.int32)
    user_vec = user_table[user_index]
    item_vec = item_table[item_index]
    user_gmf = user_vec[:, :gmf_width]
    item_gmf = item_vec[:, :gmf_width]
    user_mlp = user_vec[:, gmf_width:]
    item_mlp = item_vec[:, gmf_width:]
    h_user = jnp.dot(user_mlp, w1_user, preferred_element_type=jnp.float32).astype(jnp.bfloat16)
    h_item = jnp.dot(item_mlp, w1_item, preferred_element_type=jnp.float32).astype(jnp.bfloat16)
    pre_one = h_user.astype(jnp.float32) + h_item.astype(jnp.float32)
    act_one = jax.nn.silu(pre_one).astype(jnp.bfloat16)
    pre_two = jnp.dot(act_one, w2_weight, preferred_element_type=jnp.float32)
    act_two = jax.nn.silu(pre_two).astype(jnp.bfloat16)
    pre_three = jnp.dot(act_two, w3_weight, preferred_element_type=jnp.float32)
    act_three = jax.nn.silu(pre_three).astype(jnp.bfloat16)
    w_gmf = w_out[:gmf_width]
    w_deep = w_out[gmf_width:]
    gmf_prod = user_gmf.astype(jnp.float32) * item_gmf.astype(jnp.float32)
    logit = jnp.sum(gmf_prod * w_gmf[None, :], axis=1) + jnp.sum(act_three.astype(jnp.float32) * w_deep[None, :], axis=1)
    delta = jax.nn.sigmoid(logit) - labels.astype(jnp.float32)
    d_three = (delta[:, None] * w_deep[None, :] * silu_slope(pre_three)).astype(jnp.bfloat16)
    d_two = (jnp.dot(d_three, w3_weight.T, preferred_element_type=jnp.float32) * silu_slope(pre_two)).astype(jnp.bfloat16)
    d_one = (jnp.dot(d_two, w2_weight.T, preferred_element_type=jnp.float32) * silu_slope(pre_one)).astype(jnp.bfloat16)
    user_gmf_grad = (delta[:, None] * w_gmf[None, :] * item_gmf.astype(jnp.float32)).astype(jnp.bfloat16)
    item_gmf_grad = (delta[:, None] * w_gmf[None, :] * user_gmf.astype(jnp.float32)).astype(jnp.bfloat16)
    user_mlp_grad = jnp.dot(d_one, w1_user.T, preferred_element_type=jnp.float32).astype(jnp.bfloat16)
    item_mlp_grad = jnp.dot(d_one, w1_item.T, preferred_element_type=jnp.float32).astype(jnp.bfloat16)
    group = ((jnp.arange(TOTAL_PAIRS, dtype=jnp.int32) // PAIRS_DEV) % N_DP).astype(jnp.int32)
    user_terms = jnp.concatenate([user_gmf_grad, user_mlp_grad], axis=1).astype(jnp.float32)
    item_terms = jnp.concatenate([item_gmf_grad, item_mlp_grad], axis=1).astype(jnp.float32)
    user_grad = jax.ops.segment_sum(user_terms, group * USERS + user_index, num_segments=N_DP * USERS).reshape(N_DP, USERS, -1)
    item_grad = jax.ops.segment_sum(item_terms, group * ITEMS + item_index, num_segments=N_DP * ITEMS).reshape(N_DP, ITEMS, -1)
    grad_w1_user = jnp.dot(user_mlp.T, d_one, preferred_element_type=jnp.float32) / PAIRS_DEV
    grad_w1_item = jnp.dot(item_mlp.T, d_one, preferred_element_type=jnp.float32) / PAIRS_DEV
    grad_w2 = jnp.dot(act_one.T, d_two, preferred_element_type=jnp.float32) / PAIRS_DEV
    grad_w3 = jnp.dot(act_two.T, d_three, preferred_element_type=jnp.float32) / PAIRS_DEV
    grad_out = jnp.concatenate([jnp.sum(delta[:, None] * gmf_prod, axis=0), jnp.sum(delta[:, None] * act_three.astype(jnp.float32), axis=0)]) / PAIRS_DEV
    return user_grad, item_grad, grad_w1_user, grad_w1_item, grad_w2, grad_w3, grad_out
```

```python
import functools

import jax
import jax.numpy as jnp
from jax import lax
from jax.experimental import pallas as pl
from jax.experimental.pallas import tpu as pltpu
from jax.sharding import PartitionSpec as P

D = 256
BF, F32, I32 = jnp.bfloat16, jnp.float32, jnp.int32
ROWS = ("emb", "dp")
PARAMS = pltpu.CompilerParams(vmem_limit_bytes=56 << 20)
W1U, W1I, W2, W3, WO, WEND = 0, 256, 512, 1024, 1536, 1600
PARTS = ((W1U, 32), (W1I, 32), (W2, 64), (W3, 64), (WO, 8))
CHUNK = 200


def dot_nn(a, b):
    return jnp.dot(a, b, preferred_element_type=F32)


def dot_nt(a, b):
    return lax.dot_general(a, b, (((1,), (1,)), ((), ())), preferred_element_type=F32)


def dot_tn(a, b):
    return lax.dot_general(a, b, (((0,), (0,)), ((), ())), preferred_element_type=F32)


def pick_rows(col, k):
    shape = (col.shape[0], k)
    return jnp.where(lax.broadcasted_iota(I32, shape, 1) == col, 1.0, 0.0).astype(BF)


def put_rows(lane, first, m):
    shape = (m, lane.shape[1])
    here = lax.broadcasted_iota(I32, shape, 0) + first
    return jnp.where(here == lane, 1.0, 0.0).astype(BF)


def column(packed, g):
    lane = lax.broadcasted_iota(I32, packed.shape, 1)
    return jnp.sum(jnp.where(lane == g, packed, 0), axis=1, keepdims=True)


def sigmoid(v):
    return 1.0 / (1.0 + jnp.exp(-v))


def silu_pair(z):
    sig = sigmoid(z)
    return (z * sig).astype(BF), (sig * (1.0 + z * (1.0 - sig))).astype(BF)


def arrange_kernel(cap, uo_ref, ur_ref, io_ref, ir_ref, lab_ref, req_ref, lanes_ref, cols_ref):
    blocks = uo_ref.shape[0]
    owners = 16
    upto = jnp.where(
        lax.broadcasted_iota(I32, (128, 128), 0) <= lax.broadcasted_iota(I32, (128, 128), 1),
        1.0, 0.0,
    ).astype(BF)

    def ranks(owner):
        chosen = [
            jnp.where(
                lax.broadcasted_iota(I32, (owners, 128), 0) == owner[j : j + 1, :], 1.0, 0.0
            )
            for j in range(blocks)
        ]
        running = dot_nn(jnp.concatenate(chosen, axis=0).astype(BF), upto)
        before = jnp.zeros((owners, 1), F32)
        places = []
        for j in range(blocks):
            run = running[j * owners : (j + 1) * owners]
            places.append(
                jnp.sum(chosen[j] * (run + (before - 1.0)), axis=0, keepdims=True)
            )
            before = before + run[:, 127:128]
        return chosen, places

    def split(v):
        high = v >> 6
        return high.astype(F32), (v - (high << 6)).astype(F32)

    def spread(chosen, values):
        return jnp.concatenate(
            [c * v for c, v in zip(chosen, values)], axis=1
        ).astype(BF)

    def slots_of(places):
        sub = lax.broadcasted_iota(I32, (256, 128), 0)
        return jnp.concatenate(
            [jnp.where(sub == p.astype(I32), 1.0, 0.0) for p in places], axis=1
        ).astype(BF)

    uo, ur, io, ir, lab = (r[...] for r in (uo_ref, ur_ref, io_ref, ir_ref, lab_ref))
    u_chosen, u_places = ranks(uo)
    i_chosen, i_places = ranks(io)
    u_slots, i_slots = slots_of(u_places), slots_of(i_places)

    def rows(v):
        return [v[j : j + 1] for j in range(blocks)]

    ur_hi, ur_lo = split(ur)
    ir_hi, ir_lo = split(ir)
    item_slot = [
        io[j : j + 1] * cap + i_places[j].astype(I32) for j in range(blocks)
    ]
    is_hi, is_lo = split(jnp.concatenate(item_slot, axis=0))
    flag = (lab + 1).astype(F32)

    def wanted(chosen, slots, hi, lo):
        return dot_nt(spread(chosen, rows(hi)), slots) * 64.0 + dot_nt(
            spread(chosen, rows(lo)), slots
        )

    req_ref[:, 0:256] = wanted(u_chosen, u_slots, ur_hi, ur_lo).astype(I32)
    req_ref[:, 256:512] = wanted(i_chosen, i_slots, ir_hi, ir_lo).astype(I32)
    s_hi, s_lo = spread(u_chosen, rows(is_hi)), spread(u_chosen, rows(is_lo))
    s_flag = spread(u_chosen, rows(flag))
    lanes_ref[...] = (dot_nt(s_hi, u_slots) * 64.0 + dot_nt(s_lo, u_slots)).astype(I32)
    cols_ref[0] = (dot_nt(u_slots, s_hi) * 64.0 + dot_nt(u_slots, s_lo)).astype(I32)
    cols_ref[1] = dot_nt(u_slots, s_flag).astype(I32)


def fetch_kernel(wcol_ref, ut_ref, it_ref, out_ref):
    g = pl.program_id(0)
    groups = pl.num_programs(0)
    peers, both, width = out_ref.shape
    cap = both // 2
    for t, table in enumerate((ut_ref, it_ref)):
        col = column(wcol_ref[...], g + t * groups)
        got = dot_nn(pick_rows(col, table.shape[0]), table[...]).astype(BF)
        out_ref[:, t * cap : (t + 1) * cap, :] = got.reshape(peers, cap, width)


def forward_kernel(
    icol_ref, um_ref, im_ref, w1u_ref, w1i_ref, w2_ref, w3_ref, wo_ref,
    im_out, a1_out, s1_out, a2_out, s2_out, a3_out, s3_out, deep_out,
):
    g = pl.program_id(0)
    m = um_ref.shape[0] * um_ref.shape[1]
    slots = im_ref.shape[0] * im_ref.shape[1]
    um = um_ref[...].reshape(m, D)
    sel = pick_rows(column(icol_ref[...], g), slots)
    im = dot_nn(sel, im_ref[...].reshape(slots, D)).astype(BF)
    im_out[...] = im
    z1 = dot_nn(um, w1u_ref[...]).astype(BF).astype(F32) + dot_nn(im, w1i_ref[...]).astype(
        BF
    ).astype(F32)
    a1, s1 = silu_pair(z1)
    a1_out[...], s1_out[...] = a1, s1
    a2, s2 = silu_pair(dot_nn(a1, w2_ref[...]))
    a2_out[...], s2_out[...] = a2, s2
    a3, s3 = silu_pair(dot_nn(a2, w3_ref[...]))
    a3_out[...], s3_out[...] = a3, s3
    deep = jnp.sum(a3.astype(F32) * wo_ref[:, D:], axis=1, keepdims=True)
    deep_out[...] = jnp.broadcast_to(deep, deep_out.shape)


def middle_kernel(
    icol_ref, fcol_ref, ilane_ref, ug_ref, ig_ref, deep_ref, wo_ref,
    out_ref, delta_out, go_out, gi_scr,
):
    step = pl.program_id(0)
    groups = pl.num_programs(0) // 2
    peers, cap, _ = ug_ref.shape
    m = peers * cap
    slots = ig_ref.shape[0] * cap

    @pl.when(step < groups)
    def _():
        ug = ug_ref[...].reshape(m, D).astype(F32)
        sel = pick_rows(column(icol_ref[...], step), slots)
        ig = dot_nn(sel, ig_ref[...].reshape(slots, D))
        wg = wo_ref[:, :D]
        prod = ug * ig
        logit = jnp.sum(prod * wg, axis=1, keepdims=True) + deep_ref[:, 0:1]
        flag = column(fcol_ref[...], step)
        delta = sigmoid(logit) - (flag - 1).astype(F32)
        delta = jnp.where(flag > 0, delta, 0.0)
        delta_out[...] = jnp.broadcast_to(delta, delta_out.shape)
        dw = delta * wg
        out_ref[...] = (dw * ig).astype(BF).reshape(peers, cap, D)
        gi_scr[pl.ds(pl.multiple_of(step * m, m), m), :] = (dw * ug).astype(BF)
        part = jnp.sum(delta * prod, axis=0, keepdims=True)

        @pl.when(step == 0)
        def _():
            go_out[...] = part

        @pl.when(step > 0)
        def _():
            go_out[...] += part

    @pl.when(step >= groups)
    def _():
        sel = put_rows(ilane_ref[...], (step - groups) * m, m)
        out_ref[...] = dot_nn(sel, gi_scr[...]).astype(BF).reshape(peers, cap, D)


def backward_kernel(
    me_ref, delta_ref, um_ref, im_ref, a1_ref, s1_ref, a2_ref, s2_ref, a3_ref, s3_ref,
    w1u_ref, w1i_ref, w2_ref, w3_ref, wo_ref, go_ref,
    mu_out, mi_out, *rest,
):
    *chunks, gw_out = rest
    step = pl.program_id(0)
    m = um_ref.shape[0] * um_ref.shape[1]
    um = um_ref[...].reshape(m, D)
    delta = delta_ref[:, 0:1]

    @pl.when(step == 0)
    def _():
        gw_out[...] = jnp.zeros_like(gw_out)
        gw_out[WO : WO + 1, 0:D] = go_ref[...]

    d3 = (delta * wo_ref[:, D:] * s3_ref[...].astype(F32)).astype(BF)
    d2 = (dot_nt(d3, w3_ref[...]) * s2_ref[...].astype(F32)).astype(BF)
    d1 = (dot_nt(d2, w2_ref[...]) * s1_ref[...].astype(F32)).astype(BF)
    mu_out[...] = dot_nt(d1, w1u_ref[...]).astype(BF).reshape(mu_out.shape)
    mi_out[...] = dot_nt(d1, w1i_ref[...]).astype(BF)
    gw_out[W1U:W1I, :] += dot_tn(um, d1)
    gw_out[W1I:W2, :] += dot_tn(im_ref[...], d1)
    gw_out[W2:W3, :] += dot_tn(a1_ref[...], d2)
    gw_out[W3:WO, :] += dot_tn(a2_ref[...], d3)
    gw_out[WO + 1 : WO + 2, :] += jnp.sum(
        delta * a3_ref[...].astype(F32), axis=0, keepdims=True
    )

    @pl.when(step == pl.num_programs(0) - 1)
    def _():
        for k, chunk in enumerate(chunks):
            peer = (me_ref[0] + k) % len(chunks)
            at = 0
            for first, count in PARTS:
                start = pl.multiple_of(first + peer * count, 8)
                chunk[at : at + count, :] = gw_out[pl.ds(start, count), :].astype(BF)
                at += count


def assemble_kernel(scale, me_ref, *refs):
    chunks, outs = refs[:8], refs[8:]
    for k, chunk in enumerate(chunks):
        peer = (me_ref[0] + 8 - k) % 8
        at = 0
        for (_, count), out in zip(PARTS, outs):
            rows = chunk[at : at + count, :].astype(F32) * scale
            out[pl.ds(pl.multiple_of(peer * count, 8), count), :] = rows
            at += count


def place_kernel(ilane_ref, mi_ref, _, out_ref):
    peers, cap, _ = out_ref.shape
    m = peers * cap
    sel = put_rows(ilane_ref[...], pl.program_id(0) * m, m)
    out_ref[...] = dot_nn(sel, mi_ref[...]).astype(BF).reshape(peers, cap, D)


def gather_add_kernel(lane_ref, terms_ref, *rest):
    out_ref = rest[-1]
    m = out_ref.shape[0]
    slots = terms_ref.shape[0] * terms_ref.shape[1]
    sel = put_rows(lane_ref[...], pl.program_id(0) * m, m)
    out_ref[...] = dot_nn(sel, terms_ref[...].reshape(slots, D))


def whole(shape):
    return pl.BlockSpec(shape, lambda i: (0,) * len(shape))


def body(
    user_table, item_table, user_owner, user_row, item_owner, item_row, labels,
    w1_user, w1_item, w2_weight, w3_weight, w_out,
):
    owners = lax.axis_size("emb")
    pairs = labels.shape[0]
    rows = user_table.shape[0]
    cap = 3 * pairs // (2 * owners)
    slots = owners * cap
    groups = 4
    peers = owners // groups
    m = peers * cap
    hid = w2_weight.shape[0]
    blocks = pairs // 128
    wo = w_out.reshape(1, -1)

    def call(kernel, grid, in_specs, out_specs, out_shape, scratch=(), aliases=None, flops=0, moved=0):
        return pl.pallas_call(
            kernel, grid=grid, in_specs=in_specs, out_specs=out_specs, out_shape=out_shape,
            scratch_shapes=scratch, input_output_aliases=aliases or {}, compiler_params=PARAMS,
            cost_estimate=pl.CostEstimate(flops=flops, bytes_accessed=moved, transcendentals=0),
        )

    def exchange(x):
        return lax.all_to_all(x, "emb", split_axis=0, concat_axis=0, tiled=True)

    req, lanes, cols = pl.pallas_call(
        functools.partial(arrange_kernel, cap),
        out_shape=(
            jax.ShapeDtypeStruct((owners, 512), I32),
            jax.ShapeDtypeStruct((owners, 256), I32),
            jax.ShapeDtypeStruct((2, 256, owners), I32),
        ),
        compiler_params=PARAMS,
    )(*(a.reshape(blocks, 128) for a in (user_owner, user_row, item_owner, item_row, labels)))

    wanted = exchange(req).reshape(owners, 2, 256)[:, :, :cap]
    wcol = wanted.reshape(groups, peers, 2, cap).transpose(1, 3, 2, 0).reshape(m, 2 * groups)
    wlane = wanted.transpose(1, 0, 2).reshape(2, 1, slots)
    ilane = lanes[:, :cap].reshape(1, slots)
    side = cols[:, :cap, :].reshape(2, cap, groups, peers).transpose(0, 3, 1, 2)
    side = side.reshape(2, m, groups)
    icol, fcol = side[0], side[1]

    buffer = jax.ShapeDtypeStruct((owners, 2 * cap, D), BF)
    user_block = pl.BlockSpec((peers, cap, D), lambda i: (i, 0, 0))
    all_items = pl.BlockSpec((owners, cap, D), lambda i: (0, 1, 0))
    tile = pl.BlockSpec((m, hid), lambda i: (i, 0))
    narrow = pl.BlockSpec((m, D), lambda i: (i, 0))
    thin = pl.BlockSpec((m, 128), lambda i: (i, 0))
    weights = [whole((D, hid)), whole((D, hid)), whole((hid, hid)), whole((hid, hid))]
    wide = jax.ShapeDtypeStruct((slots, hid), BF)
    pick = 2 * slots * slots * D

    def fetch(half):
        table = pl.BlockSpec((rows, D), lambda i: (0, half))
        return call(
            fetch_kernel, (groups,), [whole((m, 2 * groups)), table, table],
            pl.BlockSpec((peers, 2 * cap, D), lambda i: (i, 0, 0)), buffer,
            flops=4 * slots * rows * D, moved=4 * slots * D + 4 * rows * D,
        )(wcol, user_table, item_table)

    mlp_back = exchange(fetch(1))
    gmf_back = exchange(fetch(0))

    im, a1, s1, a2, s2, a3, s3, deep = call(
        forward_kernel, (groups,),
        [whole((m, groups)), user_block, all_items, *weights, whole((1, D + hid))],
        [narrow, tile, tile, tile, tile, tile, tile, thin],
        [jax.ShapeDtypeStruct((slots, D), BF)] + [wide] * 6 + [jax.ShapeDtypeStruct((slots, 128), F32)],
        flops=pick + 2 * slots * hid * (2 * D + 2 * hid), moved=16 * slots * hid,
    )(icol, mlp_back, mlp_back, w1_user, w1_item, w2_weight, w3_weight, wo)

    last = groups - 1
    gmf_out, delta, go = call(
        middle_kernel, (2 * groups,),
        [
            whole((m, groups)), whole((m, groups)), whole((1, slots)),
            pl.BlockSpec((peers, cap, D), lambda i: (jnp.minimum(i, last), 0, 0)), all_items,
            pl.BlockSpec((m, 128), lambda i: (jnp.minimum(i, last), 0)), whole((1, D + hid)),
        ],
        [
            pl.BlockSpec((peers, cap, D), lambda i: (i % groups, i // groups, 0)),
            pl.BlockSpec((m, 128), lambda i: (jnp.minimum(i, last), 0)), whole((1, D)),
        ],
        [buffer, jax.ShapeDtypeStruct((slots, 128), F32), jax.ShapeDtypeStruct((1, D), F32)],
        scratch=[pltpu.VMEM((slots, D), BF)], flops=2 * pick, moved=12 * slots * D,
    )(icol, fcol, ilane, gmf_back, gmf_back, deep, wo)

    gmf_terms = exchange(gmf_out)

    me = lax.axis_index("dp").astype(I32).reshape(1)
    n_dp = lax.axis_size("dp")
    scalar = pl.BlockSpec(memory_space=pltpu.SMEM)
    piece = jax.ShapeDtypeStruct((CHUNK, hid), BF)
    mu_out, mi, *pieces = call(
        backward_kernel, (groups,),
        [scalar, thin, user_block, narrow, tile, tile, tile, tile, tile, tile, *weights,
         whole((1, D + hid)), whole((1, D))],
        [user_block, narrow] + [whole((CHUNK, hid))] * n_dp,
        [buffer, jax.ShapeDtypeStruct((slots, D), BF)] + [piece] * n_dp,
        scratch=[pltpu.VMEM((WEND, hid), F32)],
        flops=4 * slots * hid * (2 * D + 2 * hid), moved=16 * slots * hid,
    )(me, delta, mlp_back, im, a1, s1, a2, s2, a3, s3, w1_user, w1_item, w2_weight, w3_weight, wo, go)

    mlp_out = call(
        place_kernel, (groups,),
        [whole((1, slots)), whole((slots, D)), pl.BlockSpec(memory_space=pl.ANY)],
        pl.BlockSpec((peers, cap, D), lambda i: (i, 1, 0)), buffer, aliases={2: 0},
        flops=pick, moved=4 * slots * D,
    )(ilane, mi, mu_out)

    mlp_terms = exchange(mlp_out)

    def shift_dp(x, k):
        return lax.ppermute(x, "dp", [(s, (s + k) % n_dp) for s in range(n_dp)])

    def shift_emb(x, kx, kz):
        side = 4
        return lax.ppermute(
            x, "emb",
            [
                (a * side + b, (a + kx) % side * side + (b + kz) % side)
                for a in range(side) for b in range(side)
            ],
        )

    def ring_sum(v, step):
        v = v.astype(BF)
        one, two, three = (step(v, k).astype(F32) for k in (1, 2, 3))
        return (v.astype(F32) + two) + (one + three)

    part = pieces[0].astype(F32)
    for k in range(1, n_dp):
        part = part + shift_dp(pieces[k], k).astype(F32)
    part = ring_sum(part, lambda v, k: shift_emb(v, k, 0))
    part = ring_sum(part, lambda v, k: shift_emb(v, 0, k)).astype(BF)
    found = [part] + [shift_dp(part, k) for k in range(1, n_dp)]
    gw1u, gw1i, gw2, gw3, gwo = pl.pallas_call(
        functools.partial(assemble_kernel, 1.0 / pairs),
        in_specs=[scalar] + [pl.BlockSpec(memory_space=pltpu.VMEM)] * n_dp,
        out_shape=[jax.ShapeDtypeStruct((count * n_dp, hid), F32) for _, count in PARTS],
        compiler_params=PARAMS,
    )(me, *found)

    def gather_add(terms, t, half, into=None):
        r = rows // 2
        return call(
            gather_add_kernel, (rows // r,),
            [whole((1, slots)), pl.BlockSpec((owners, cap, D), lambda i: (0, t, 0))]
            + ([] if into is None else [pl.BlockSpec(memory_space=pl.ANY)]),
            pl.BlockSpec((r, D), lambda i: (i, half)),
            jax.ShapeDtypeStruct((rows, 2 * D), F32),
            aliases=None if into is None else {2: 0},
            flops=2 * rows * slots * D, moved=2 * slots * D + 4 * rows * D,
        )(wlane[t], terms, *(() if into is None else (into,)))

    grads = [gather_add(gmf_terms, t, 0) for t in (0, 1)]
    user_grad, item_grad = (gather_add(mlp_terms, t, 1, grads[t]) for t in (0, 1))
    grad_out = jnp.concatenate([gwo[0, :D], gwo[1]])
    return user_grad[None], item_grad[None], gw1u, gw1i, gw2, gw3, grad_out


def solution(mesh):
    return jax.shard_map(
        body,
        mesh=mesh,
        in_specs=(
            P("emb", None), P("emb", None), P(ROWS, None), P(ROWS), P(ROWS, None), P(ROWS), P(ROWS),
            P(), P(), P(), P(), P(),
        ),
        out_specs=(P("dp", "emb", None), P("dp", "emb", None), P(), P(), P(), P(), P()),
        check_vma=False,
    )
```

```python
import functools

import jax
import jax.numpy as jnp
from jax import lax
from jax.experimental import pallas as pl
from jax.experimental.pallas import tpu as pltpu
from jax.sharding import PartitionSpec as P

D = 256
BF, F32, I32 = jnp.bfloat16, jnp.float32, jnp.int32
ROWS = ("emb", "dp")


PARAMS = pltpu.CompilerParams(vmem_limit_bytes=56 << 20)


W1U, W1I, W2, W3, WO, WEND = 0, 256, 512, 1024, 1536, 1600
PARTS = ((W1U, 32), (W1I, 32), (W2, 64), (W3, 64), (WO, 8))
CHUNK, HALF = 200, 104


def dot_nn(a, b):
    return jnp.dot(a, b, preferred_element_type=F32)


def dot_nt(a, b):
    return lax.dot_general(a, b, (((1,), (1,)), ((), ())), preferred_element_type=F32)


def dot_tn(a, b):
    return lax.dot_general(a, b, (((0,), (0,)), ((), ())), preferred_element_type=F32)


def pick_rows(col, k):
    shape = (col.shape[0], k)
    return jnp.where(lax.broadcasted_iota(I32, shape, 1) == col, 1.0, 0.0).astype(BF)


def put_rows(lane, first, m):
    shape = (m, lane.shape[1])
    here = lax.broadcasted_iota(I32, shape, 0) + first
    return jnp.where(here == lane, 1.0, 0.0).astype(BF)


def column(packed, g):
    lane = lax.broadcasted_iota(I32, packed.shape, 1)
    return jnp.sum(jnp.where(lane == g, packed, 0), axis=1, keepdims=True)


def sigmoid(v):
    return 1.0 / (1.0 + jnp.exp(-v))


def silu_pair(z):
    sig = sigmoid(z)
    return (z * sig).astype(BF), (sig * (1.0 + z * (1.0 - sig))).astype(BF)


def arrange_kernel(cap, uo_ref, ur_ref, io_ref, ir_ref, lab_ref, req_ref, lanes_ref, cols_ref):
    blocks = uo_ref.shape[0]
    owners = 16
    upto = jnp.where(
        lax.broadcasted_iota(I32, (128, 128), 0) <= lax.broadcasted_iota(I32, (128, 128), 1),
        1.0, 0.0,
    ).astype(BF)

    def ranks(owner):
        chosen = [
            jnp.where(
                lax.broadcasted_iota(I32, (owners, 128), 0) == owner[j : j + 1, :], 1.0, 0.0
            )
            for j in range(blocks)
        ]
        running = dot_nn(jnp.concatenate(chosen, axis=0).astype(BF), upto)
        before = jnp.zeros((owners, 1), F32)
        places = []
        for j in range(blocks):
            run = running[j * owners : (j + 1) * owners]
            places.append(
                jnp.sum(chosen[j] * (run + (before - 1.0)), axis=0, keepdims=True)
            )
            before = before + run[:, 127:128]
        return chosen, places

    def split(v):
        high = v >> 6
        return high.astype(F32), (v - (high << 6)).astype(F32)

    def spread(chosen, values):
        return jnp.concatenate(
            [c * v for c, v in zip(chosen, values)], axis=1
        ).astype(BF)

    def slots_of(places):
        sub = lax.broadcasted_iota(I32, (256, 128), 0)
        return jnp.concatenate(
            [jnp.where(sub == p.astype(I32), 1.0, 0.0) for p in places], axis=1
        ).astype(BF)

    uo, ur, io, ir, lab = (r[...] for r in (uo_ref, ur_ref, io_ref, ir_ref, lab_ref))
    u_chosen, u_places = ranks(uo)
    i_chosen, i_places = ranks(io)
    u_slots, i_slots = slots_of(u_places), slots_of(i_places)

    def rows(v):
        return [v[j : j + 1] for j in range(blocks)]

    ur_hi, ur_lo = split(ur)
    ir_hi, ir_lo = split(ir)
    item_slot = [
        io[j : j + 1] * cap + i_places[j].astype(I32) for j in range(blocks)
    ]
    is_hi, is_lo = split(jnp.concatenate(item_slot, axis=0))
    flag = (lab + 1).astype(F32)

    def wanted(chosen, slots, hi, lo):
        return dot_nt(spread(chosen, rows(hi)), slots) * 64.0 + dot_nt(
            spread(chosen, rows(lo)), slots
        )

    req_ref[:, 0:256] = wanted(u_chosen, u_slots, ur_hi, ur_lo).astype(I32)
    req_ref[:, 256:512] = wanted(i_chosen, i_slots, ir_hi, ir_lo).astype(I32)
    s_hi, s_lo = spread(u_chosen, rows(is_hi)), spread(u_chosen, rows(is_lo))
    s_flag = spread(u_chosen, rows(flag))
    lanes_ref[...] = (dot_nt(s_hi, u_slots) * 64.0 + dot_nt(s_lo, u_slots)).astype(I32)
    cols_ref[0] = (dot_nt(u_slots, s_hi) * 64.0 + dot_nt(u_slots, s_lo)).astype(I32)
    cols_ref[1] = dot_nt(u_slots, s_flag).astype(I32)


def fetch_kernel(wcol_ref, ut_ref, it_ref, out_ref):
    g = pl.program_id(0)
    groups = pl.num_programs(0)
    peers, both, width = out_ref.shape
    cap = both // 2
    for t, table in enumerate((ut_ref, it_ref)):
        col = column(wcol_ref[...], g + t * groups)
        got = dot_nn(pick_rows(col, table.shape[0]), table[...]).astype(BF)
        out_ref[:, t * cap : (t + 1) * cap, :] = got.reshape(peers, cap, width)


def forward_kernel(
    icol_ref, um_ref, im_ref, w1u_ref, w1i_ref, w2_ref, w3_ref, wo_ref,
    im_out, a1_out, s1_out, a2_out, s2_out, a3_out, s3_out, deep_out,
):
    g = pl.program_id(0)
    m = um_ref.shape[0] * um_ref.shape[1]
    slots = im_ref.shape[0] * im_ref.shape[1]
    um = um_ref[...].reshape(m, D)
    sel = pick_rows(column(icol_ref[...], g), slots)
    im = dot_nn(sel, im_ref[...].reshape(slots, D)).astype(BF)
    im_out[...] = im
    z1 = dot_nn(um, w1u_ref[...]).astype(BF).astype(F32) + dot_nn(im, w1i_ref[...]).astype(
        BF
    ).astype(F32)
    a1, s1 = silu_pair(z1)
    a1_out[...], s1_out[...] = a1, s1
    a2, s2 = silu_pair(dot_nn(a1, w2_ref[...]))
    a2_out[...], s2_out[...] = a2, s2
    a3, s3 = silu_pair(dot_nn(a2, w3_ref[...]))
    a3_out[...], s3_out[...] = a3, s3
    deep = jnp.sum(a3.astype(F32) * wo_ref[:, D:], axis=1, keepdims=True)
    deep_out[...] = jnp.broadcast_to(deep, deep_out.shape)


def middle_kernel(
    icol_ref, fcol_ref, ilane_ref, ug_ref, ig_ref, deep_ref, wo_ref,
    out_ref, delta_out, go_out, gi_scr,
):
    step = pl.program_id(0)
    groups = pl.num_programs(0) // 2
    peers, cap, _ = ug_ref.shape
    m = peers * cap
    slots = ig_ref.shape[0] * cap

    @pl.when(step < groups)
    def _():
        ug = ug_ref[...].reshape(m, D).astype(F32)
        sel = pick_rows(column(icol_ref[...], step), slots)
        ig = dot_nn(sel, ig_ref[...].reshape(slots, D))
        wg = wo_ref[:, :D]
        prod = ug * ig
        logit = jnp.sum(prod * wg, axis=1, keepdims=True) + deep_ref[:, 0:1]
        flag = column(fcol_ref[...], step)
        delta = sigmoid(logit) - (flag - 1).astype(F32)
        delta = jnp.where(flag > 0, delta, 0.0)
        delta_out[...] = jnp.broadcast_to(delta, delta_out.shape)
        dw = delta * wg
        out_ref[...] = (dw * ig).astype(BF).reshape(peers, cap, D)
        gi_scr[pl.ds(pl.multiple_of(step * m, m), m), :] = (dw * ug).astype(BF)
        part = jnp.sum(delta * prod, axis=0, keepdims=True)

        @pl.when(step == 0)
        def _():
            go_out[...] = part

        @pl.when(step > 0)
        def _():
            go_out[...] += part

    @pl.when(step >= groups)
    def _():
        sel = put_rows(ilane_ref[...], (step - groups) * m, m)
        out_ref[...] = dot_nn(sel, gi_scr[...]).astype(BF).reshape(peers, cap, D)


def backward_kernel(
    me_ref, delta_ref, um_ref, im_ref, a1_ref, s1_ref, a2_ref, s2_ref, a3_ref, s3_ref,
    w2_ref, w3_ref, wo_ref, go_ref, d1_out, keep_out, give_out, gw_ref,
):
    step = pl.program_id(0)
    m = um_ref.shape[0] * um_ref.shape[1]
    um = um_ref[...].reshape(m, D)
    delta = delta_ref[:, 0:1]

    @pl.when(step == 0)
    def _():
        gw_ref[...] = jnp.zeros_like(gw_ref)
        gw_ref[WO : WO + 1, 0:D] = go_ref[...]

    d3 = (delta * wo_ref[:, D:] * s3_ref[...].astype(F32)).astype(BF)
    d2 = (dot_nt(d3, w3_ref[...]) * s2_ref[...].astype(F32)).astype(BF)
    d1 = (dot_nt(d2, w2_ref[...]) * s1_ref[...].astype(F32)).astype(BF)
    d1_out[...] = d1
    gw_ref[W1U:W1I, :] += dot_tn(um, d1)
    gw_ref[W1I:W2, :] += dot_tn(im_ref[...], d1)
    gw_ref[W2:W3, :] += dot_tn(a1_ref[...], d2)
    gw_ref[W3:WO, :] += dot_tn(a2_ref[...], d3)
    gw_ref[WO + 1 : WO + 2, :] += jnp.sum(
        delta * a3_ref[...].astype(F32), axis=0, keepdims=True
    )

    @pl.when(step == pl.num_programs(0) - 1)
    def _():
        y, core = me_ref[0] // 2, me_ref[0] % 2
        for half, out in ((core, keep_out), (1 - core, give_out)):
            at = 0
            for j in range(4):
                peer = (y + j) % 4 * 2 + half
                for first, count in PARTS:
                    start = pl.multiple_of(first + peer * count, 8)
                    out[at : at + count, :] = gw_ref[pl.ds(start, count), :].astype(BF)
                    at += count


def rows_kernel(ilane_ref, d1_ref, w1u_ref, w1i_ref, out_ref, mi_scr):
    step = pl.program_id(0)
    groups = pl.num_programs(0) // 2
    peers, cap, _ = out_ref.shape
    m = peers * cap

    @pl.when(step < groups)
    def _():
        d1 = d1_ref[...]
        out_ref[...] = dot_nt(d1, w1u_ref[...]).astype(BF).reshape(peers, cap, D)
        mi_scr[pl.ds(pl.multiple_of(step * m, m), m), :] = dot_nt(d1, w1i_ref[...]).astype(BF)

    @pl.when(step >= groups)
    def _():
        sel = put_rows(ilane_ref[...], (step - groups) * m, m)
        out_ref[...] = dot_nn(sel, mi_scr[...]).astype(BF).reshape(peers, cap, D)


def assemble_kernel(scale, me_ref, *refs):
    chunks, outs = refs[:8], refs[8:]
    y, core = me_ref[0] // 2, me_ref[0] % 2
    for k, chunk in enumerate(chunks):
        half = core if k < 4 else 1 - core
        peer = (y + 4 - k % 4) % 4 * 2 + half
        at = 0
        for (_, count), out in zip(PARTS, outs):
            rows = chunk[at : at + count, :].astype(F32) * scale
            out[pl.ds(pl.multiple_of(peer * count, 8), count), :] = rows
            at += count


def gather_add_kernel(lane_ref, terms_ref, *rest):
    out_ref = rest[-1]
    m = out_ref.shape[0]
    slots = terms_ref.shape[0] * terms_ref.shape[1]
    sel = put_rows(lane_ref[...], pl.program_id(0) * m, m)
    out_ref[...] = dot_nn(sel, terms_ref[...].reshape(slots, D))


def whole(shape):
    return pl.BlockSpec(shape, lambda i: (0,) * len(shape))


def body(
    user_table, item_table, user_owner, user_row, item_owner, item_row, labels,
    w1_user, w1_item, w2_weight, w3_weight, w_out,
):
    owners = lax.axis_size("emb")
    pairs = labels.shape[0]
    rows = user_table.shape[0]
    cap = 3 * pairs // (2 * owners)
    slots = owners * cap
    groups = 4
    peers = owners // groups
    m = peers * cap
    hid = w2_weight.shape[0]
    blocks = pairs // 128
    wo = w_out.reshape(1, -1)

    def call(kernel, grid, in_specs, out_specs, out_shape, scratch=(), aliases=None, flops=0, moved=0):
        return pl.pallas_call(
            kernel, grid=grid, in_specs=in_specs, out_specs=out_specs, out_shape=out_shape,
            scratch_shapes=scratch, input_output_aliases=aliases or {}, compiler_params=PARAMS,
            cost_estimate=pl.CostEstimate(flops=flops // 64, bytes_accessed=moved // 64, transcendentals=0),
        )

    def exchange(x):
        return lax.all_to_all(x, "emb", split_axis=0, concat_axis=0, tiled=True)

    req, lanes, cols = pl.pallas_call(
        functools.partial(arrange_kernel, cap),
        out_shape=(
            jax.ShapeDtypeStruct((owners, 512), I32),
            jax.ShapeDtypeStruct((owners, 256), I32),
            jax.ShapeDtypeStruct((2, 256, owners), I32),
        ),
        compiler_params=PARAMS,
    )(*(a.reshape(blocks, 128) for a in (user_owner, user_row, item_owner, item_row, labels)))

    wanted = exchange(req).reshape(owners, 2, 256)[:, :, :cap]
    wcol = wanted.reshape(groups, peers, 2, cap).transpose(1, 3, 2, 0).reshape(m, 2 * groups)
    wlane = wanted.transpose(1, 0, 2).reshape(2, 1, slots)
    ilane = lanes[:, :cap].reshape(1, slots)
    side = cols[:, :cap, :].reshape(2, cap, groups, peers).transpose(0, 3, 1, 2)
    side = side.reshape(2, m, groups)
    icol, fcol = side[0], side[1]

    buffer = jax.ShapeDtypeStruct((owners, 2 * cap, D), BF)
    user_block = pl.BlockSpec((peers, cap, D), lambda i: (i, 0, 0))
    all_items = pl.BlockSpec((owners, cap, D), lambda i: (0, 1, 0))
    tile = pl.BlockSpec((m, hid), lambda i: (i, 0))
    narrow = pl.BlockSpec((m, D), lambda i: (i, 0))
    thin = pl.BlockSpec((m, 128), lambda i: (i, 0))
    weights = [whole((D, hid)), whole((D, hid)), whole((hid, hid)), whole((hid, hid))]
    wide = jax.ShapeDtypeStruct((slots, hid), BF)
    pick = 2 * slots * slots * D

    def fetch(half):
        table = pl.BlockSpec((rows, D), lambda i: (0, half))
        return call(
            fetch_kernel, (groups,), [whole((m, 2 * groups)), table, table],
            pl.BlockSpec((peers, 2 * cap, D), lambda i: (i, 0, 0)), buffer,
            flops=4 * slots * rows * D, moved=4 * slots * D + 4 * rows * D,
        )(wcol, user_table, item_table)

    mlp_back = exchange(fetch(1))
    gmf_back = exchange(fetch(0))

    im, a1, s1, a2, s2, a3, s3, deep = call(
        forward_kernel, (groups,),
        [whole((m, groups)), user_block, all_items, *weights, whole((1, D + hid))],
        [narrow, tile, tile, tile, tile, tile, tile, thin],
        [jax.ShapeDtypeStruct((slots, D), BF)] + [wide] * 6 + [jax.ShapeDtypeStruct((slots, 128), F32)],
        flops=pick + 2 * slots * hid * (2 * D + 2 * hid), moved=16 * slots * hid,
    )(icol, mlp_back, mlp_back, w1_user, w1_item, w2_weight, w3_weight, wo)

    last = groups - 1
    gmf_out, delta, go = call(
        middle_kernel, (2 * groups,),
        [
            whole((m, groups)), whole((m, groups)), whole((1, slots)),
            pl.BlockSpec((peers, cap, D), lambda i: (jnp.minimum(i, last), 0, 0)), all_items,
            pl.BlockSpec((m, 128), lambda i: (jnp.minimum(i, last), 0)), whole((1, D + hid)),
        ],
        [
            pl.BlockSpec((peers, cap, D), lambda i: (i % groups, i // groups, 0)),
            pl.BlockSpec((m, 128), lambda i: (jnp.minimum(i, last), 0)), whole((1, D)),
        ],
        [buffer, jax.ShapeDtypeStruct((slots, 128), F32), jax.ShapeDtypeStruct((1, D), F32)],
        scratch=[pltpu.VMEM((slots, D), BF)], flops=2 * pick, moved=12 * slots * D,
    )(icol, fcol, ilane, gmf_back, gmf_back, deep, wo)

    gmf_terms = exchange(gmf_out)

    me = lax.axis_index("dp").astype(I32).reshape(1)
    n_dp = lax.axis_size("dp")
    scalar = pl.BlockSpec(memory_space=pltpu.SMEM)
    stack = jax.ShapeDtypeStruct((4 * CHUNK, hid), BF)
    d1, keep, give = call(
        backward_kernel, (groups,),
        [scalar, thin, user_block, narrow, tile, tile, tile, tile, tile, tile,
         whole((hid, hid)), whole((hid, hid)), whole((1, D + hid)), whole((1, D))],
        [tile, whole((4 * CHUNK, hid)), whole((4 * CHUNK, hid))], [wide, stack, stack],
        scratch=[pltpu.VMEM((WEND, hid), F32)],
        flops=2 * slots * hid * (2 * D + 4 * hid), moved=16 * slots * hid,
    )(me, delta, mlp_back, im, a1, s1, a2, s2, a3, s3, w2_weight, w3_weight, wo, go)

    mlp_out = call(
        rows_kernel, (2 * groups,),
        [whole((1, slots)), pl.BlockSpec((m, hid), lambda i: (jnp.minimum(i, last), 0)),
         whole((D, hid)), whole((D, hid))],
        pl.BlockSpec((peers, cap, D), lambda i: (i % groups, i // groups, 0)), buffer,
        scratch=[pltpu.VMEM((slots, D), BF)], flops=pick + 4 * slots * hid * D,
        moved=4 * slots * hid,
    )(ilane, d1, w1_user, w1_item)

    def gather_add(terms, t, half, into=None):
        r = rows // 2
        return call(
            gather_add_kernel, (rows // r,),
            [whole((1, slots)), pl.BlockSpec((owners, cap, D), lambda i: (0, t, 0))]
            + ([] if into is None else [pl.BlockSpec(memory_space=pl.ANY)]),
            pl.BlockSpec((r, D), lambda i: (i, half)),
            jax.ShapeDtypeStruct((rows, 2 * D), F32),
            aliases=None if into is None else {2: 0},
            flops=2 * rows * slots * D, moved=2 * slots * D + 4 * rows * D,
        )(wlane[t], terms, *(() if into is None else (into,)))

    def shift_dp(x, k):
        return lax.ppermute(x, "dp", [(s, (s + k) % n_dp) for s in range(n_dp)])

    def shift_emb(x, kx, kz):
        side = 4
        return lax.ppermute(
            x, "emb",
            [
                (a * side + b, (a + kx) % side * side + (b + kz) % side)
                for a in range(side) for b in range(side)
            ],
        )

    def ring_sum(v, step):
        v = v.astype(BF)
        one, two, three = (step(v, k).astype(F32) for k in (1, 2, 3))
        return (v.astype(F32) + two) + (one + three)

    def swap_core(x):
        return lax.ppermute(x, "dp", [(s, s ^ 1) for s in range(n_dp)])

    got = swap_core(give)
    both = [
        keep[j * CHUNK : (j + 1) * CHUNK].astype(F32) + got[j * CHUNK : (j + 1) * CHUNK].astype(F32)
        for j in range(4)
    ]
    part = both[0]
    for j in range(1, 4):
        part = part + shift_dp(both[j].astype(BF), 2 * j).astype(F32)
    mlp_out, part = lax.optimization_barrier((mlp_out, part))

    def over_x(v, k):
        return shift_emb(v, k, 0)

    def over_z(v, k):
        return shift_emb(v, 0, k)

    top, low = part[:HALF], part[HALF:]
    top, low = ring_sum(top, over_x), ring_sum(low, over_z)
    top, low = ring_sum(top, over_z), ring_sum(low, over_x)
    mlp_out, top, low = lax.optimization_barrier((mlp_out, top, low))
    mlp_terms = exchange(mlp_out)
    part = jnp.concatenate([top, low]).astype(BF)
    user_grad = gather_add(gmf_terms, 0, 0)
    item_grad = gather_add(gmf_terms, 1, 0)
    found = [part] + [shift_dp(part, 2 * j) for j in range(1, 4)]
    found = found + [swap_core(v) for v in found]
    gw1u, gw1i, gw2, gw3, gwo = pl.pallas_call(
        functools.partial(assemble_kernel, 1.0 / pairs),
        in_specs=[scalar] + [pl.BlockSpec(memory_space=pltpu.VMEM)] * n_dp,
        out_shape=[jax.ShapeDtypeStruct((count * n_dp, hid), F32) for _, count in PARTS],
        compiler_params=PARAMS,
    )(me, *found)

    mlp_terms, user_grad, item_grad, gw1u, gw1i, gw2, gw3, gwo = lax.optimization_barrier(
        (mlp_terms, user_grad, item_grad, gw1u, gw1i, gw2, gw3, gwo)
    )
    user_grad = gather_add(mlp_terms, 0, 1, user_grad)
    item_grad = gather_add(mlp_terms, 1, 1, item_grad)
    grad_out = jnp.concatenate([gwo[0, :D], gwo[1]])
    return user_grad[None], item_grad[None], gw1u, gw1i, gw2, gw3, grad_out


def solution(mesh):
    return jax.shard_map(
        body,
        mesh=mesh,
        in_specs=(
            P("emb", None), P("emb", None), P(ROWS, None), P(ROWS), P(ROWS, None), P(ROWS), P(ROWS),
            P(), P(), P(), P(), P(),
        ),
        out_specs=(P("dp", "emb", None), P("dp", "emb", None), P(), P(), P(), P(), P()),
        check_vma=False,
    )
```

```python
import functools

import jax
import jax.numpy as jnp
from jax import lax
from jax.experimental import pallas as pl
from jax.experimental.pallas import tpu as pltpu
from jax.sharding import PartitionSpec as P

D = 256
BF, F32, I32 = jnp.bfloat16, jnp.float32, jnp.int32
ROWS = ("emb", "dp")


PARAMS = pltpu.CompilerParams(vmem_limit_bytes=63 << 20)


W1U, W1I, W2, W3, WO, WEND = 0, 256, 512, 1024, 1536, 1600
PARTS = ((W1U, 32), (W1I, 32), (W2, 64), (W3, 64), (WO, 8))
CHUNK, HALF = 200, 104


def dot_nn(a, b):
    return jnp.dot(a, b, preferred_element_type=F32)


def dot_nt(a, b):
    return lax.dot_general(a, b, (((1,), (1,)), ((), ())), preferred_element_type=F32)


def dot_tn(a, b):
    return lax.dot_general(a, b, (((0,), (0,)), ((), ())), preferred_element_type=F32)


def pick_rows(col, k):
    shape = (col.shape[0], k)
    return jnp.where(lax.broadcasted_iota(I32, shape, 1) == col, 1.0, 0.0).astype(BF)


def put_rows(lane, first, m):
    shape = (m, lane.shape[1])
    here = lax.broadcasted_iota(I32, shape, 0) + first
    return jnp.where(here == lane, 1.0, 0.0).astype(BF)


def column(packed, g):
    lane = lax.broadcasted_iota(I32, packed.shape, 1)
    return jnp.sum(jnp.where(lane == g, packed, 0), axis=1, keepdims=True)


def sigmoid(v):
    return 1.0 / (1.0 + jnp.exp(-v))


def silu_pair(z):
    sig = sigmoid(z)
    return (z * sig).astype(BF), (sig * (1.0 + z * (1.0 - sig))).astype(BF)


def arrange_kernel(cap, uo_ref, ur_ref, io_ref, ir_ref, lab_ref, req_ref, lanes_ref, cols_ref):
    blocks = uo_ref.shape[0]
    owners = 16
    upto = jnp.where(
        lax.broadcasted_iota(I32, (128, 128), 0) <= lax.broadcasted_iota(I32, (128, 128), 1),
        1.0, 0.0,
    ).astype(BF)

    def ranks(owner):
        chosen = [
            jnp.where(
                lax.broadcasted_iota(I32, (owners, 128), 0) == owner[j : j + 1, :], 1.0, 0.0
            )
            for j in range(blocks)
        ]
        running = dot_nn(jnp.concatenate(chosen, axis=0).astype(BF), upto)
        before = jnp.zeros((owners, 1), F32)
        places = []
        for j in range(blocks):
            run = running[j * owners : (j + 1) * owners]
            places.append(
                jnp.sum(chosen[j] * (run + (before - 1.0)), axis=0, keepdims=True)
            )
            before = before + run[:, 127:128]
        return chosen, places

    def split(v):
        high = v >> 6
        return high.astype(F32), (v - (high << 6)).astype(F32)

    def spread(chosen, values):
        return jnp.concatenate(
            [c * v for c, v in zip(chosen, values)], axis=1
        ).astype(BF)

    def slots_of(places):
        sub = lax.broadcasted_iota(I32, (256, 128), 0)
        return jnp.concatenate(
            [jnp.where(sub == p.astype(I32), 1.0, 0.0) for p in places], axis=1
        ).astype(BF)

    uo, ur, io, ir, lab = (r[...] for r in (uo_ref, ur_ref, io_ref, ir_ref, lab_ref))
    u_chosen, u_places = ranks(uo)
    i_chosen, i_places = ranks(io)
    u_slots, i_slots = slots_of(u_places), slots_of(i_places)

    def rows(v):
        return [v[j : j + 1] for j in range(blocks)]

    ur_hi, ur_lo = split(ur)
    ir_hi, ir_lo = split(ir)
    item_slot = [
        io[j : j + 1] * cap + i_places[j].astype(I32) for j in range(blocks)
    ]
    is_hi, is_lo = split(jnp.concatenate(item_slot, axis=0))
    flag = (lab + 1).astype(F32)

    def wanted(chosen, slots, hi, lo):
        return dot_nt(spread(chosen, rows(hi)), slots) * 64.0 + dot_nt(
            spread(chosen, rows(lo)), slots
        )

    req = jnp.concatenate(
        [wanted(u_chosen, u_slots, ur_hi, ur_lo), wanted(i_chosen, i_slots, ir_hi, ir_lo)], axis=1
    ).astype(I32)
    for o in range(owners):
        req_ref[o] = req[o : o + 1]
    s_hi, s_lo = spread(u_chosen, rows(is_hi)), spread(u_chosen, rows(is_lo))
    s_flag = spread(u_chosen, rows(flag))
    lanes_ref[...] = (dot_nt(s_hi, u_slots) * 64.0 + dot_nt(s_lo, u_slots)).astype(I32)
    cols_ref[0] = (dot_nt(u_slots, s_hi) * 64.0 + dot_nt(u_slots, s_lo)).astype(I32)
    cols_ref[1] = dot_nt(u_slots, s_flag).astype(I32)


def fetch_kernel(asked_ref, ut_ref, it_ref, out_ref):
    peers, both, width = out_ref.shape
    cap = both // 2
    first = pl.program_id(0) * peers
    rows = [asked_ref[first + q] for q in range(peers)]
    for t, table in enumerate((ut_ref, it_ref)):
        lanes = jnp.concatenate([r[:, t * 256 : (t + 1) * 256] for r in rows + rows], axis=0)
        cols = jnp.transpose(lanes)
        col = jnp.concatenate([cols[:cap, q : q + 1] for q in range(peers)], axis=0)
        got = dot_nn(pick_rows(col, table.shape[0]), table[...]).astype(BF)
        out_ref[:, t * cap : (t + 1) * cap, :] = got.reshape(peers, cap, width)


def forward_kernel(
    icol_ref, um_ref, im_ref, w1u_ref, w1i_ref, w2_ref, w3_ref, wo_ref,
    im_out, a1_out, s1_out, a2_out, s2_out, a3_out, s3_out, deep_out,
):
    g = pl.program_id(0)
    m = um_ref.shape[0] * um_ref.shape[1]
    slots = im_ref.shape[0] * im_ref.shape[1]
    um = um_ref[...].reshape(m, D)
    sel = pick_rows(column(icol_ref[...], g), slots)
    im = dot_nn(sel, im_ref[...].reshape(slots, D)).astype(BF)
    im_out[...] = im
    z1 = dot_nn(um, w1u_ref[...]).astype(BF).astype(F32) + dot_nn(im, w1i_ref[...]).astype(
        BF
    ).astype(F32)
    a1, s1 = silu_pair(z1)
    a1_out[...], s1_out[...] = a1, s1
    a2, s2 = silu_pair(dot_nn(a1, w2_ref[...]))
    a2_out[...], s2_out[...] = a2, s2
    a3, s3 = silu_pair(dot_nn(a2, w3_ref[...]))
    a3_out[...], s3_out[...] = a3, s3
    deep = jnp.sum(a3.astype(F32) * wo_ref[:, D:], axis=1, keepdims=True)
    deep_out[...] = jnp.broadcast_to(deep, deep_out.shape)


def middle_kernel(
    icol_ref, fcol_ref, ilane_ref, ug_ref, ig_ref, deep_ref, wo_ref,
    out_ref, delta_out, go_out, gi_scr,
):
    step = pl.program_id(0)
    groups = pl.num_programs(0) // 2
    peers, cap, _ = ug_ref.shape
    m = peers * cap
    slots = ig_ref.shape[0] * cap

    @pl.when(step < groups)
    def _():
        ug = ug_ref[...].reshape(m, D).astype(F32)
        sel = pick_rows(column(icol_ref[...], step), slots)
        ig = dot_nn(sel, ig_ref[...].reshape(slots, D))
        wg = wo_ref[:, :D]
        prod = ug * ig
        logit = jnp.sum(prod * wg, axis=1, keepdims=True) + deep_ref[:, 0:1]
        flag = column(fcol_ref[...], step)
        delta = sigmoid(logit) - (flag - 1).astype(F32)
        delta = jnp.where(flag > 0, delta, 0.0)
        delta_out[...] = jnp.broadcast_to(delta, delta_out.shape)
        dw = delta * wg
        out_ref[...] = (dw * ig).astype(BF).reshape(peers, cap, D)
        gi_scr[pl.ds(pl.multiple_of(step * m, m), m), :] = (dw * ug).astype(BF)
        part = jnp.sum(delta * prod, axis=0, keepdims=True)

        @pl.when(step == 0)
        def _():
            go_out[...] = part

        @pl.when(step > 0)
        def _():
            go_out[...] += part

    @pl.when(step >= groups)
    def _():
        sel = put_rows(ilane_ref[...], (step - groups) * m, m)
        out_ref[...] = dot_nn(sel, gi_scr[...]).astype(BF).reshape(peers, cap, D)


def backward_kernel(
    me_ref, delta_ref, um_ref, im_ref, a1_ref, s1_ref, a2_ref, s2_ref, a3_ref, s3_ref,
    w2_ref, w3_ref, wo_ref, go_ref, d1_out, keep_out, give_out, gw_ref,
):
    step = pl.program_id(0)
    m = um_ref.shape[0] * um_ref.shape[1]
    um = um_ref[...].reshape(m, D)
    delta = delta_ref[:, 0:1]

    @pl.when(step == 0)
    def _():
        gw_ref[...] = jnp.zeros_like(gw_ref)
        gw_ref[WO : WO + 1, 0:D] = go_ref[...]

    d3 = (delta * wo_ref[:, D:] * s3_ref[...].astype(F32)).astype(BF)
    d2 = (dot_nt(d3, w3_ref[...]) * s2_ref[...].astype(F32)).astype(BF)
    d1 = (dot_nt(d2, w2_ref[...]) * s1_ref[...].astype(F32)).astype(BF)
    d1_out[...] = d1
    gw_ref[W1U:W1I, :] += dot_tn(um, d1)
    gw_ref[W1I:W2, :] += dot_tn(im_ref[...], d1)
    gw_ref[W2:W3, :] += dot_tn(a1_ref[...], d2)
    gw_ref[W3:WO, :] += dot_tn(a2_ref[...], d3)
    gw_ref[WO + 1 : WO + 2, :] += jnp.sum(
        delta * a3_ref[...].astype(F32), axis=0, keepdims=True
    )

    @pl.when(step == pl.num_programs(0) - 1)
    def _():
        y, core = me_ref[0] // 2, me_ref[0] % 2
        for half, out in ((core, keep_out), (1 - core, give_out)):
            at = 0
            for j in range(4):
                peer = (y + j) % 4 * 2 + half
                for first, count in PARTS:
                    start = pl.multiple_of(first + peer * count, 8)
                    out[at : at + count, :] = gw_ref[pl.ds(start, count), :].astype(BF)
                    at += count


def rows_kernel(ilane_ref, d1_ref, w1u_ref, w1i_ref, out_ref, mi_scr):
    step = pl.program_id(0)
    groups = pl.num_programs(0) // 2
    peers, cap, _ = out_ref.shape
    m = peers * cap

    @pl.when(step < groups)
    def _():
        d1 = d1_ref[...]
        out_ref[...] = dot_nt(d1, w1u_ref[...]).astype(BF).reshape(peers, cap, D)
        mi_scr[pl.ds(pl.multiple_of(step * m, m), m), :] = dot_nt(d1, w1i_ref[...]).astype(BF)

    @pl.when(step >= groups)
    def _():
        sel = put_rows(ilane_ref[...], (step - groups) * m, m)
        out_ref[...] = dot_nn(sel, mi_scr[...]).astype(BF).reshape(peers, cap, D)


def assemble_kernel(scale, me_ref, *refs):
    chunks, outs = refs[:8], refs[8:]
    y, core = me_ref[0] // 2, me_ref[0] % 2
    for k, chunk in enumerate(chunks):
        half = core if k < 4 else 1 - core
        peer = (y + 4 - k % 4) % 4 * 2 + half
        at = 0
        for (_, count), out in zip(PARTS, outs):
            rows = chunk[at : at + count, :].astype(F32) * scale
            out[pl.ds(pl.multiple_of(peer * count, 8), count), :] = rows
            at += count


def gather_add_kernel(lane_ref, terms_ref, *rest):
    user_out, item_out = rest[-2:]
    step = pl.program_id(0)
    steps = pl.num_programs(0) // 2
    m = user_out.shape[0]
    slots = terms_ref.shape[0] * terms_ref.shape[1]
    sel = put_rows(lane_ref[0], step % steps * m, m)
    got = dot_nn(sel, terms_ref[...].reshape(slots, D))

    @pl.when(step < steps)
    def _():
        user_out[...] = got

    @pl.when(step >= steps)
    def _():
        item_out[...] = got


def whole(shape):
    return pl.BlockSpec(shape, lambda i: (0,) * len(shape))


def body(
    user_table, item_table, user_owner, user_row, item_owner, item_row, labels,
    w1_user, w1_item, w2_weight, w3_weight, w_out,
):
    owners = lax.axis_size("emb")
    pairs = labels.shape[0]
    rows = user_table.shape[0]
    cap = 3 * pairs // (2 * owners)
    slots = owners * cap
    groups = 4
    peers = owners // groups
    m = peers * cap
    hid = w2_weight.shape[0]
    blocks = pairs // 128
    wo = w_out.reshape(1, -1)

    def call(kernel, grid, in_specs, out_specs, out_shape, scratch=(), aliases=None, flops=0, moved=0):
        return pl.pallas_call(
            kernel, grid=grid, in_specs=in_specs, out_specs=out_specs, out_shape=out_shape,
            scratch_shapes=scratch, input_output_aliases=aliases or {}, compiler_params=PARAMS,
            cost_estimate=pl.CostEstimate(flops=flops // 64, bytes_accessed=moved // 64, transcendentals=0),
        )

    def exchange(x):
        return lax.all_to_all(x, "emb", split_axis=0, concat_axis=0, tiled=True)

    req, lanes, cols = pl.pallas_call(
        functools.partial(arrange_kernel, cap),
        out_shape=(
            jax.ShapeDtypeStruct((owners, 1, 512), I32),
            jax.ShapeDtypeStruct((owners, 256), I32),
            jax.ShapeDtypeStruct((2, 256, owners), I32),
        ),
        compiler_params=PARAMS,
    )(*(a.reshape(blocks, 128) for a in (user_owner, user_row, item_owner, item_row, labels)))

    asked = exchange(req)
    wanted = asked.reshape(owners, 2, 256)[:, :, :cap]
    wlane = wanted.transpose(1, 0, 2).reshape(2, 1, slots)
    ilane = lanes[:, :cap].reshape(1, slots)
    side = cols[:, :cap, :].reshape(2, cap, groups, peers).transpose(0, 3, 1, 2)
    side = side.reshape(2, m, groups)
    icol, fcol = side[0], side[1]

    buffer = jax.ShapeDtypeStruct((owners, 2 * cap, D), BF)
    user_block = pl.BlockSpec((peers, cap, D), lambda i: (i, 0, 0))
    all_items = pl.BlockSpec((owners, cap, D), lambda i: (0, 1, 0))
    tile = pl.BlockSpec((m, hid), lambda i: (i, 0))
    narrow = pl.BlockSpec((m, D), lambda i: (i, 0))
    thin = pl.BlockSpec((m, 128), lambda i: (i, 0))
    weights = [whole((D, hid)), whole((D, hid)), whole((hid, hid)), whole((hid, hid))]
    wide = jax.ShapeDtypeStruct((slots, hid), BF)
    pick = 2 * slots * slots * D

    def fetch(half):
        table = pl.BlockSpec((rows, D), lambda i: (0, half))
        return call(
            fetch_kernel, (groups,), [whole((owners, 1, 512)), table, table],
            pl.BlockSpec((peers, 2 * cap, D), lambda i: (i, 0, 0)), buffer,
            flops=4 * slots * rows * D, moved=4 * slots * D + 4 * rows * D,
        )(asked, user_table, item_table)

    mlp_back = exchange(fetch(1))
    gmf_back = exchange(fetch(0))

    im, a1, s1, a2, s2, a3, s3, deep = call(
        forward_kernel, (groups,),
        [whole((m, groups)), user_block, all_items, *weights, whole((1, D + hid))],
        [narrow, tile, tile, tile, tile, tile, tile, thin],
        [jax.ShapeDtypeStruct((slots, D), BF)] + [wide] * 6 + [jax.ShapeDtypeStruct((slots, 128), F32)],
        flops=pick + 2 * slots * hid * (2 * D + 2 * hid), moved=16 * slots * hid,
    )(icol, mlp_back, mlp_back, w1_user, w1_item, w2_weight, w3_weight, wo)

    last = groups - 1
    gmf_out, delta, go = call(
        middle_kernel, (2 * groups,),
        [
            whole((m, groups)), whole((m, groups)), whole((1, slots)),
            pl.BlockSpec((peers, cap, D), lambda i: (jnp.minimum(i, last), 0, 0)), all_items,
            pl.BlockSpec((m, 128), lambda i: (jnp.minimum(i, last), 0)), whole((1, D + hid)),
        ],
        [
            pl.BlockSpec((peers, cap, D), lambda i: (i % groups, i // groups, 0)),
            pl.BlockSpec((m, 128), lambda i: (jnp.minimum(i, last), 0)), whole((1, D)),
        ],
        [buffer, jax.ShapeDtypeStruct((slots, 128), F32), jax.ShapeDtypeStruct((1, D), F32)],
        scratch=[pltpu.VMEM((slots, D), BF)], flops=2 * pick, moved=12 * slots * D,
    )(icol, fcol, ilane, gmf_back, gmf_back, deep, wo)

    gmf_terms = exchange(gmf_out)

    me = lax.axis_index("dp").astype(I32).reshape(1)
    n_dp = lax.axis_size("dp")
    scalar = pl.BlockSpec(memory_space=pltpu.SMEM)
    stack = jax.ShapeDtypeStruct((4 * CHUNK, hid), BF)
    fine = groups
    small_tile = pl.BlockSpec((slots // fine, hid), lambda i: (i, 0))
    d1, keep, give = call(
        backward_kernel, (fine,),
        [scalar, pl.BlockSpec((slots // fine, 128), lambda i: (i, 0)),
         pl.BlockSpec((owners // fine, cap, D), lambda i: (i, 0, 0)),
         pl.BlockSpec((slots // fine, D), lambda i: (i, 0)), *[small_tile] * 6,
         whole((hid, hid)), whole((hid, hid)), whole((1, D + hid)), whole((1, D))],
        [small_tile, whole((4 * CHUNK, hid)), whole((4 * CHUNK, hid))], [wide, stack, stack],
        scratch=[pltpu.VMEM((WEND, hid), F32)],
        flops=2 * slots * hid * (2 * D + 4 * hid), moved=16 * slots * hid,
    )(me, delta, mlp_back, im, a1, s1, a2, s2, a3, s3, w2_weight, w3_weight, wo, go)

    mlp_out = call(
        rows_kernel, (2 * groups,),
        [whole((1, slots)), pl.BlockSpec((m, hid), lambda i: (jnp.minimum(i, last), 0)),
         whole((D, hid)), whole((D, hid))],
        pl.BlockSpec((peers, cap, D), lambda i: (i % groups, i // groups, 0)), buffer,
        scratch=[pltpu.VMEM((slots, D), BF)], flops=pick + 4 * slots * hid * D,
        moved=4 * slots * hid,
    )(ilane, d1, w1_user, w1_item)

    def gather_add(terms, half, *into):
        steps = 4
        r = rows // steps
        grad = jax.ShapeDtypeStruct((rows, 2 * D), F32)
        return call(
            gather_add_kernel, (2 * steps,),
            [pl.BlockSpec((1, 1, slots), lambda i: (i // steps, 0, 0)),
             pl.BlockSpec((owners, cap, D), lambda i: (0, i // steps, 0))]
            + [pl.BlockSpec(memory_space=pl.ANY)] * len(into),
            [pl.BlockSpec((r, D), lambda i: (jnp.minimum(i, steps - 1), half)),
             pl.BlockSpec((r, D), lambda i: (jnp.maximum(i - steps, 0), half))],
            [grad, grad], aliases={2 + k: k for k in range(len(into))},
            flops=4 * rows * slots * D, moved=4 * slots * D + 8 * rows * D,
        )(wlane, terms, *into)

    def shift_dp(x, k):
        return lax.ppermute(x, "dp", [(s, (s + k) % n_dp) for s in range(n_dp)])

    def shift_emb(x, kx, kz):
        side = 4
        return lax.ppermute(
            x, "emb",
            [
                (a * side + b, (a + kx) % side * side + (b + kz) % side)
                for a in range(side) for b in range(side)
            ],
        )

    def ring_sum(v, step):
        v = v.astype(BF)
        one, two, three = (step(v, k).astype(F32) for k in (1, 2, 3))
        return (v.astype(F32) + two) + (one + three)

    def swap_core(x):
        return lax.ppermute(x, "dp", [(s, s ^ 1) for s in range(n_dp)])

    got = swap_core(give)
    both = [
        keep[j * CHUNK : (j + 1) * CHUNK].astype(F32) + got[j * CHUNK : (j + 1) * CHUNK].astype(F32)
        for j in range(4)
    ]
    part = both[0]
    for j in range(1, 4):
        part = part + shift_dp(both[j].astype(BF), 2 * j).astype(F32)
    mlp_out, part = lax.optimization_barrier((mlp_out, part))

    def over_x(v, k):
        return shift_emb(v, k, 0)

    def over_z(v, k):
        return shift_emb(v, 0, k)

    top, low = part[:HALF], part[HALF:]
    top, low = ring_sum(top, over_x), ring_sum(low, over_z)
    top, low = ring_sum(top, over_z), ring_sum(low, over_x)
    mlp_out, top, low = lax.optimization_barrier((mlp_out, top, low))
    mlp_terms = exchange(mlp_out)
    part = jnp.concatenate([top, low]).astype(BF)
    user_grad, item_grad = gather_add(gmf_terms, 0)
    found = [part] + [shift_dp(part, 2 * j) for j in range(1, 4)]
    found = found + [swap_core(v) for v in found]
    gw1u, gw1i, gw2, gw3, gwo = pl.pallas_call(
        functools.partial(assemble_kernel, 1.0 / pairs),
        in_specs=[scalar] + [pl.BlockSpec(memory_space=pltpu.VMEM)] * n_dp,
        out_shape=[jax.ShapeDtypeStruct((count * n_dp, hid), F32) for _, count in PARTS],
        compiler_params=PARAMS,
    )(me, *found)

    grad_out = jnp.concatenate([gwo[0, :D], gwo[1]])
    mlp_terms, user_grad, item_grad, grad_out = lax.optimization_barrier(
        (mlp_terms, user_grad, item_grad, grad_out)
    )
    user_grad, item_grad = gather_add(mlp_terms, 1, user_grad, item_grad)
    return user_grad[None], item_grad[None], gw1u, gw1i, gw2, gw3, grad_out


def solution(mesh):
    return jax.shard_map(
        body,
        mesh=mesh,
        in_specs=(
            P("emb", None), P("emb", None), P(ROWS, None), P(ROWS), P(ROWS, None), P(ROWS), P(ROWS),
            P(), P(), P(), P(), P(),
        ),
        out_specs=(P("dp", "emb", None), P("dp", "emb", None), P(), P(), P(), P(), P()),
        check_vma=False,
    )
```

```python
import functools

import jax
import jax.numpy as jnp
from jax import lax
from jax.experimental import pallas as pl
from jax.experimental.pallas import tpu as pltpu
from jax.sharding import PartitionSpec as P

D = 256
BF, F32, I32 = jnp.bfloat16, jnp.float32, jnp.int32
ROWS = ("emb", "dp")


PARAMS = pltpu.CompilerParams(vmem_limit_bytes=63 << 20)


W1U, W1I, W2, W3, WO, WEND = 0, 256, 512, 1024, 1536, 1600
PARTS = ((W1U, 32), (W1I, 32), (W2, 64), (W3, 64), (WO, 8))
CHUNK, HALF = 200, 104


def dot_nn(a, b):
    return jnp.dot(a, b, preferred_element_type=F32)


def dot_nt(a, b):
    return lax.dot_general(a, b, (((1,), (1,)), ((), ())), preferred_element_type=F32)


def dot_tn(a, b):
    return lax.dot_general(a, b, (((0,), (0,)), ((), ())), preferred_element_type=F32)


def pick_rows(col, k):
    shape = (col.shape[0], k)
    return jnp.where(lax.broadcasted_iota(I32, shape, 1) == col, 1.0, 0.0).astype(BF)


def put_rows(lane, first, m):
    shape = (m, lane.shape[1])
    here = lax.broadcasted_iota(I32, shape, 0) + first
    return jnp.where(here == lane, 1.0, 0.0).astype(BF)


def column(packed, g):
    lane = lax.broadcasted_iota(I32, packed.shape, 1)
    return jnp.sum(jnp.where(lane == g, packed, 0), axis=1, keepdims=True)


def sigmoid(v):
    return 1.0 / (1.0 + jnp.exp(-v))


def silu_pair(z):
    sig = sigmoid(z)
    return (z * sig).astype(BF), (sig * (1.0 + z * (1.0 - sig))).astype(BF)


def arrange_kernel(cap, uo_ref, ur_ref, io_ref, ir_ref, lab_ref, req_ref, lanes_ref, cols_ref):
    blocks = uo_ref.shape[0]
    owners = 16
    upto = jnp.where(
        lax.broadcasted_iota(I32, (128, 128), 0) <= lax.broadcasted_iota(I32, (128, 128), 1),
        1.0, 0.0,
    ).astype(BF)

    def ranks(owner):
        chosen = [
            jnp.where(
                lax.broadcasted_iota(I32, (owners, 128), 0) == owner[j : j + 1, :], 1.0, 0.0
            )
            for j in range(blocks)
        ]
        running = dot_nn(jnp.concatenate(chosen, axis=0).astype(BF), upto)
        before = jnp.zeros((owners, 1), F32)
        places = []
        for j in range(blocks):
            run = running[j * owners : (j + 1) * owners]
            places.append(
                jnp.sum(chosen[j] * (run + (before - 1.0)), axis=0, keepdims=True)
            )
            before = before + run[:, 127:128]
        return chosen, places

    def split(v):
        high = v >> 6
        return high.astype(F32), (v - (high << 6)).astype(F32)

    def spread(chosen, values):
        return jnp.concatenate(
            [c * v for c, v in zip(chosen, values)], axis=1
        ).astype(BF)

    def slots_of(places):
        sub = lax.broadcasted_iota(I32, (256, 128), 0)
        return jnp.concatenate(
            [jnp.where(sub == p.astype(I32), 1.0, 0.0) for p in places], axis=1
        ).astype(BF)

    uo, ur, io, ir, lab = (r[...] for r in (uo_ref, ur_ref, io_ref, ir_ref, lab_ref))
    u_chosen, u_places = ranks(uo)
    i_chosen, i_places = ranks(io)
    u_slots, i_slots = slots_of(u_places), slots_of(i_places)

    def rows(v):
        return [v[j : j + 1] for j in range(blocks)]

    ur_hi, ur_lo = split(ur)
    ir_hi, ir_lo = split(ir)
    item_slot = [
        io[j : j + 1] * cap + i_places[j].astype(I32) for j in range(blocks)
    ]
    is_hi, is_lo = split(jnp.concatenate(item_slot, axis=0))
    flag = (lab + 1).astype(F32)

    def wanted(chosen, slots, hi, lo):
        return dot_nt(spread(chosen, rows(hi)), slots) * 64.0 + dot_nt(
            spread(chosen, rows(lo)), slots
        )

    req = jnp.concatenate(
        [wanted(u_chosen, u_slots, ur_hi, ur_lo), wanted(i_chosen, i_slots, ir_hi, ir_lo)], axis=1
    ).astype(I32)
    for o in range(owners):
        req_ref[o] = req[o : o + 1]
    s_hi, s_lo = spread(u_chosen, rows(is_hi)), spread(u_chosen, rows(is_lo))
    s_flag = spread(u_chosen, rows(flag))
    lanes_ref[...] = (dot_nt(s_hi, u_slots) * 64.0 + dot_nt(s_lo, u_slots)).astype(I32)
    cols_ref[0] = (dot_nt(u_slots, s_hi) * 64.0 + dot_nt(u_slots, s_lo)).astype(I32)
    cols_ref[1] = dot_nt(u_slots, s_flag).astype(I32)


def fetch_kernel(asked_ref, ut_ref, it_ref, out_ref):
    peers, both, width = out_ref.shape
    cap = both // 2
    first = pl.program_id(0) * peers
    rows = [asked_ref[first + q] for q in range(peers)]
    for t, table in enumerate((ut_ref, it_ref)):
        lanes = jnp.concatenate([r[:, t * 256 : (t + 1) * 256] for r in rows + rows], axis=0)
        cols = jnp.transpose(lanes)
        col = jnp.concatenate([cols[:cap, q : q + 1] for q in range(peers)], axis=0)
        got = dot_nn(pick_rows(col, table.shape[0]), table[...]).astype(BF)
        out_ref[:, t * cap : (t + 1) * cap, :] = got.reshape(peers, cap, width)


def forward_kernel(
    icol_ref, um_ref, im_ref, w1u_ref, w1i_ref, w2_ref, w3_ref, wo_ref,
    im_out, a1_out, s1_out, a2_out, s2_out, a3_out, s3_out, deep_out,
):
    g = pl.program_id(0)
    m = um_ref.shape[0] * um_ref.shape[1]
    slots = im_ref.shape[0] * im_ref.shape[1]
    um = um_ref[...].reshape(m, D)
    sel = pick_rows(column(icol_ref[...], g), slots)
    im = dot_nn(sel, im_ref[...].reshape(slots, D)).astype(BF)
    im_out[...] = im
    z1 = dot_nn(um, w1u_ref[...]).astype(BF).astype(F32) + dot_nn(im, w1i_ref[...]).astype(
        BF
    ).astype(F32)
    a1, s1 = silu_pair(z1)
    a1_out[...], s1_out[...] = a1, s1
    a2, s2 = silu_pair(dot_nn(a1, w2_ref[...]))
    a2_out[...], s2_out[...] = a2, s2
    a3, s3 = silu_pair(dot_nn(a2, w3_ref[...]))
    a3_out[...], s3_out[...] = a3, s3
    deep = jnp.sum(a3.astype(F32) * wo_ref[:, D:], axis=1, keepdims=True)
    deep_out[...] = jnp.broadcast_to(deep, deep_out.shape)


def middle_kernel(
    icol_ref, fcol_ref, ug_ref, ig_ref, deep_ref, wo_ref, gu_out, gi_out, delta_out, go_out
):
    step = pl.program_id(0)
    peers, cap, _ = ug_ref.shape
    m = peers * cap
    slots = ig_ref.shape[0] * cap
    ug = ug_ref[...].reshape(m, D).astype(F32)
    sel = pick_rows(column(icol_ref[...], step), slots)
    ig = dot_nn(sel, ig_ref[...].reshape(slots, D))
    wg = wo_ref[:, :D]
    prod = ug * ig
    logit = jnp.sum(prod * wg, axis=1, keepdims=True) + deep_ref[:, 0:1]
    flag = column(fcol_ref[...], step)
    delta = sigmoid(logit) - (flag - 1).astype(F32)
    delta = jnp.where(flag > 0, delta, 0.0)
    delta_out[...] = jnp.broadcast_to(delta, delta_out.shape)
    dw = delta * wg
    gu_out[...] = (dw * ig).astype(BF).reshape(peers, cap, D)
    gi_out[...] = (dw * ug).astype(BF)
    part = jnp.sum(delta * prod, axis=0, keepdims=True)

    @pl.when(step == 0)
    def _():
        go_out[...] = part

    @pl.when(step > 0)
    def _():
        go_out[...] += part


def place_kernel(ilane_ref, g_ref, out_ref):
    peers, cap, _ = out_ref.shape
    m = peers * cap
    sel = put_rows(ilane_ref[...], pl.program_id(0) * m, m)
    out_ref[...] = dot_nn(sel, g_ref[...]).astype(BF).reshape(peers, cap, D)


def backward_kernel(
    me_ref, delta_ref, um_ref, im_ref, a1_ref, s1_ref, a2_ref, s2_ref, a3_ref, s3_ref,
    w2_ref, w3_ref, wo_ref, go_ref, d1_out, keep_out, give_out, gw_ref,
):
    step = pl.program_id(0)
    m = um_ref.shape[0] * um_ref.shape[1]
    um = um_ref[...].reshape(m, D)
    delta = delta_ref[:, 0:1]

    @pl.when(step == 0)
    def _():
        gw_ref[...] = jnp.zeros_like(gw_ref)
        gw_ref[WO : WO + 1, 0:D] = go_ref[...]

    d3 = (delta * wo_ref[:, D:] * s3_ref[...].astype(F32)).astype(BF)
    d2 = (dot_nt(d3, w3_ref[...]) * s2_ref[...].astype(F32)).astype(BF)
    d1 = (dot_nt(d2, w2_ref[...]) * s1_ref[...].astype(F32)).astype(BF)
    d1_out[...] = d1
    gw_ref[W1U:W1I, :] += dot_tn(um, d1)
    gw_ref[W1I:W2, :] += dot_tn(im_ref[...], d1)
    gw_ref[W2:W3, :] += dot_tn(a1_ref[...], d2)
    gw_ref[W3:WO, :] += dot_tn(a2_ref[...], d3)
    gw_ref[WO + 1 : WO + 2, :] += jnp.sum(
        delta * a3_ref[...].astype(F32), axis=0, keepdims=True
    )

    @pl.when(step == pl.num_programs(0) - 1)
    def _():
        y, core = me_ref[0] // 2, me_ref[0] % 2
        for half, out in ((core, keep_out), (1 - core, give_out)):
            at = 0
            for j in range(4):
                peer = (y + j) % 4 * 2 + half
                for first, count in PARTS:
                    start = pl.multiple_of(first + peer * count, 8)
                    out[at : at + count, :] = gw_ref[pl.ds(start, count), :].astype(BF)
                    at += count


def rows_kernel(ilane_ref, d1_ref, w1u_ref, w1i_ref, out_ref, mi_scr):
    step = pl.program_id(0)
    groups = pl.num_programs(0) // 2
    peers, cap, _ = out_ref.shape
    m = peers * cap

    @pl.when(step < groups)
    def _():
        d1 = d1_ref[...]
        out_ref[...] = dot_nt(d1, w1u_ref[...]).astype(BF).reshape(peers, cap, D)
        mi_scr[pl.ds(pl.multiple_of(step * m, m), m), :] = dot_nt(d1, w1i_ref[...]).astype(BF)

    @pl.when(step >= groups)
    def _():
        sel = put_rows(ilane_ref[...], (step - groups) * m, m)
        out_ref[...] = dot_nn(sel, mi_scr[...]).astype(BF).reshape(peers, cap, D)


def assemble_kernel(scale, me_ref, *refs):
    chunks, outs = refs[:8], refs[8:]
    y, core = me_ref[0] // 2, me_ref[0] % 2
    for k, chunk in enumerate(chunks):
        half = core if k < 4 else 1 - core
        peer = (y + 4 - k % 4) % 4 * 2 + half
        at = 0
        for (_, count), out in zip(PARTS, outs):
            rows = chunk[at : at + count, :].astype(F32) * scale
            out[pl.ds(pl.multiple_of(peer * count, 8), count), :] = rows
            at += count


def gather_add_kernel(lane_ref, user_ref, item_ref, *rest):
    user_out, item_out = rest[-2:]
    step = pl.program_id(0)
    steps = pl.num_programs(0) // 2
    m = user_out.shape[0]
    slots = user_ref.shape[0] * user_ref.shape[1]
    sel = put_rows(lane_ref[0], step % steps * m, m)

    @pl.when(step < steps)
    def _():
        user_out[...] = dot_nn(sel, user_ref[...].reshape(slots, D))

    @pl.when(step >= steps)
    def _():
        item_out[...] = dot_nn(sel, item_ref[...].reshape(slots, D))


def whole(shape):
    return pl.BlockSpec(shape, lambda i: (0,) * len(shape))


def body(
    user_table, item_table, user_owner, user_row, item_owner, item_row, labels,
    w1_user, w1_item, w2_weight, w3_weight, w_out,
):
    owners = lax.axis_size("emb")
    pairs = labels.shape[0]
    rows = user_table.shape[0]
    cap = 3 * pairs // (2 * owners)
    slots = owners * cap
    groups = 4
    peers = owners // groups
    m = peers * cap
    hid = w2_weight.shape[0]
    blocks = pairs // 128
    wo = w_out.reshape(1, -1)

    def call(kernel, grid, in_specs, out_specs, out_shape, scratch=(), aliases=None, flops=0, moved=0):
        return pl.pallas_call(
            kernel, grid=grid, in_specs=in_specs, out_specs=out_specs, out_shape=out_shape,
            scratch_shapes=scratch, input_output_aliases=aliases or {}, compiler_params=PARAMS,
            cost_estimate=pl.CostEstimate(flops=flops // 64, bytes_accessed=moved // 64, transcendentals=0),
        )

    def exchange(x):
        return lax.all_to_all(x, "emb", split_axis=0, concat_axis=0, tiled=True)

    req, lanes, cols = pl.pallas_call(
        functools.partial(arrange_kernel, cap),
        out_shape=(
            jax.ShapeDtypeStruct((owners, 1, 512), I32),
            jax.ShapeDtypeStruct((owners, 256), I32),
            jax.ShapeDtypeStruct((2, 256, owners), I32),
        ),
        compiler_params=PARAMS,
    )(*(a.reshape(blocks, 128) for a in (user_owner, user_row, item_owner, item_row, labels)))

    asked = exchange(req)
    wanted = asked.reshape(owners, 2, 256)[:, :, :cap]
    wlane = wanted.transpose(1, 0, 2).reshape(2, 1, slots)
    ilane = lanes[:, :cap].reshape(1, slots)
    side = cols[:, :cap, :].reshape(2, cap, groups, peers).transpose(0, 3, 1, 2)
    side = side.reshape(2, m, groups)
    icol, fcol = side[0], side[1]

    buffer = jax.ShapeDtypeStruct((owners, 2 * cap, D), BF)
    user_block = pl.BlockSpec((peers, cap, D), lambda i: (i, 0, 0))
    all_items = pl.BlockSpec((owners, cap, D), lambda i: (0, 1, 0))
    tile = pl.BlockSpec((m, hid), lambda i: (i, 0))
    narrow = pl.BlockSpec((m, D), lambda i: (i, 0))
    thin = pl.BlockSpec((m, 128), lambda i: (i, 0))
    weights = [whole((D, hid)), whole((D, hid)), whole((hid, hid)), whole((hid, hid))]
    wide = jax.ShapeDtypeStruct((slots, hid), BF)
    pick = 2 * slots * slots * D

    def fetch(half):
        table = pl.BlockSpec((rows, D), lambda i: (0, half))
        return call(
            fetch_kernel, (groups,), [whole((owners, 1, 512)), table, table],
            pl.BlockSpec((peers, 2 * cap, D), lambda i: (i, 0, 0)), buffer,
            flops=4 * slots * rows * D, moved=4 * slots * D + 4 * rows * D,
        )(asked, user_table, item_table)

    mlp_back = exchange(fetch(1))
    gmf_back = exchange(fetch(0))

    im, a1, s1, a2, s2, a3, s3, deep = call(
        forward_kernel, (groups,),
        [whole((m, groups)), user_block, all_items, *weights, whole((1, D + hid))],
        [narrow, tile, tile, tile, tile, tile, tile, thin],
        [jax.ShapeDtypeStruct((slots, D), BF)] + [wide] * 6 + [jax.ShapeDtypeStruct((slots, 128), F32)],
        flops=pick + 2 * slots * hid * (2 * D + 2 * hid), moved=16 * slots * hid,
    )(icol, mlp_back, mlp_back, w1_user, w1_item, w2_weight, w3_weight, wo)

    last = groups - 1
    single = jax.ShapeDtypeStruct((owners, cap, D), BF)
    gu_out, gi, delta, go = call(
        middle_kernel, (groups,),
        [whole((m, groups)), whole((m, groups)), user_block, all_items, thin, whole((1, D + hid))],
        [user_block, narrow, thin, whole((1, D))],
        [single, jax.ShapeDtypeStruct((slots, D), BF), jax.ShapeDtypeStruct((slots, 128), F32),
         jax.ShapeDtypeStruct((1, D), F32)],
        flops=pick, moved=12 * slots * D,
    )(icol, fcol, gmf_back, gmf_back, deep, wo)

    gu_terms = exchange(gu_out)
    gi_out = call(
        place_kernel, (groups,), [whole((1, slots)), whole((slots, D))], user_block, single,
        flops=pick, moved=4 * slots * D,
    )(ilane, gi)
    gi_out, gu_terms = lax.optimization_barrier((gi_out, gu_terms))
    gi_terms = exchange(gi_out)
    last = groups - 1

    me = lax.axis_index("dp").astype(I32).reshape(1)
    n_dp = lax.axis_size("dp")
    scalar = pl.BlockSpec(memory_space=pltpu.SMEM)
    stack = jax.ShapeDtypeStruct((4 * CHUNK, hid), BF)
    fine = groups
    small_tile = pl.BlockSpec((slots // fine, hid), lambda i: (i, 0))
    d1, keep, give = call(
        backward_kernel, (fine,),
        [scalar, pl.BlockSpec((slots // fine, 128), lambda i: (i, 0)),
         pl.BlockSpec((owners // fine, cap, D), lambda i: (i, 0, 0)),
         pl.BlockSpec((slots // fine, D), lambda i: (i, 0)), *[small_tile] * 6,
         whole((hid, hid)), whole((hid, hid)), whole((1, D + hid)), whole((1, D))],
        [small_tile, whole((4 * CHUNK, hid)), whole((4 * CHUNK, hid))], [wide, stack, stack],
        scratch=[pltpu.VMEM((WEND, hid), F32)],
        flops=2 * slots * hid * (2 * D + 4 * hid), moved=16 * slots * hid,
    )(me, delta, mlp_back, im, a1, s1, a2, s2, a3, s3, w2_weight, w3_weight, wo, go)

    mlp_out = call(
        rows_kernel, (2 * groups,),
        [whole((1, slots)), pl.BlockSpec((m, hid), lambda i: (jnp.minimum(i, last), 0)),
         whole((D, hid)), whole((D, hid))],
        pl.BlockSpec((peers, cap, D), lambda i: (i % groups, i // groups, 0)), buffer,
        scratch=[pltpu.VMEM((slots, D), BF)], flops=pick + 4 * slots * hid * D,
        moved=4 * slots * hid,
    )(ilane, d1, w1_user, w1_item)

    def gather_add(user_terms, item_terms, at, half, *into):
        steps = 4
        r = rows // steps
        grad = jax.ShapeDtypeStruct((rows, 2 * D), F32)
        return call(
            gather_add_kernel, (2 * steps,),
            [pl.BlockSpec((1, 1, slots), lambda i: (i // steps, 0, 0)),
             whole((owners, cap, D)), pl.BlockSpec((owners, cap, D), lambda i: (0, at, 0))]
            + [pl.BlockSpec(memory_space=pl.ANY)] * len(into),
            [pl.BlockSpec((r, D), lambda i: (jnp.minimum(i, steps - 1), half)),
             pl.BlockSpec((r, D), lambda i: (jnp.maximum(i - steps, 0), half))],
            [grad, grad], aliases={3 + k: k for k in range(len(into))},
            flops=4 * rows * slots * D, moved=4 * slots * D + 8 * rows * D,
        )(wlane, user_terms, item_terms, *into)

    def shift_dp(x, k):
        return lax.ppermute(x, "dp", [(s, (s + k) % n_dp) for s in range(n_dp)])

    def shift_emb(x, kx, kz):
        side = 4
        return lax.ppermute(
            x, "emb",
            [
                (a * side + b, (a + kx) % side * side + (b + kz) % side)
                for a in range(side) for b in range(side)
            ],
        )

    def ring_sum(v, step):
        v = v.astype(BF)
        one, two, three = (step(v, k).astype(F32) for k in (1, 2, 3))
        return (v.astype(F32) + two) + (one + three)

    def swap_core(x):
        return lax.ppermute(x, "dp", [(s, s ^ 1) for s in range(n_dp)])

    got = swap_core(give)
    both = [
        keep[j * CHUNK : (j + 1) * CHUNK].astype(F32) + got[j * CHUNK : (j + 1) * CHUNK].astype(F32)
        for j in range(4)
    ]
    part = both[0]
    for j in range(1, 4):
        part = part + shift_dp(both[j].astype(BF), 2 * j).astype(F32)
    mlp_out, part = lax.optimization_barrier((mlp_out, part))

    def over_x(v, k):
        return shift_emb(v, k, 0)

    def over_z(v, k):
        return shift_emb(v, 0, k)

    top, low = part[:HALF], part[HALF:]
    top, low = ring_sum(top, over_x), ring_sum(low, over_z)
    top, low = ring_sum(top, over_z), ring_sum(low, over_x)
    mlp_out, top, low = lax.optimization_barrier((mlp_out, top, low))
    mlp_terms = exchange(mlp_out)
    part = jnp.concatenate([top, low]).astype(BF)
    user_grad, item_grad = gather_add(gu_terms, gi_terms, 0, 0)
    found = [part] + [shift_dp(part, 2 * j) for j in range(1, 4)]
    found = found + [swap_core(v) for v in found]
    gw1u, gw1i, gw2, gw3, gwo = pl.pallas_call(
        functools.partial(assemble_kernel, 1.0 / pairs),
        in_specs=[scalar] + [pl.BlockSpec(memory_space=pltpu.VMEM)] * n_dp,
        out_shape=[jax.ShapeDtypeStruct((count * n_dp, hid), F32) for _, count in PARTS],
        compiler_params=PARAMS,
    )(me, *found)

    grad_out = jnp.concatenate([gwo[0, :D], gwo[1]])
    mlp_terms, user_grad, item_grad, grad_out = lax.optimization_barrier(
        (mlp_terms, user_grad, item_grad, grad_out)
    )
    user_grad, item_grad = gather_add(mlp_terms, mlp_terms, 1, 1, user_grad, item_grad)
    return user_grad[None], item_grad[None], gw1u, gw1i, gw2, gw3, grad_out


def solution(mesh):
    return jax.shard_map(
        body,
        mesh=mesh,
        in_specs=(
            P("emb", None), P("emb", None), P(ROWS, None), P(ROWS), P(ROWS, None), P(ROWS), P(ROWS),
            P(), P(), P(), P(), P(),
        ),
        out_specs=(P("dp", "emb", None), P("dp", "emb", None), P(), P(), P(), P(), P()),
        check_vma=False,
    )
```

```python
import functools

import jax
import jax.numpy as jnp
from jax import lax
from jax.experimental import pallas as pl
from jax.experimental.pallas import tpu as pltpu
from jax.sharding import PartitionSpec as P

D = 256
BF, F32, I32 = jnp.bfloat16, jnp.float32, jnp.int32
ROWS = ("emb", "dp")


PARAMS = pltpu.CompilerParams(vmem_limit_bytes=63 << 20)


W1U, W1I, W2, W3, WO, WEND = 0, 256, 512, 1024, 1536, 1600
PARTS = ((W1U, 32), (W1I, 32), (W2, 64), (W3, 64), (WO, 8))
CHUNK, HALF = 200, 104


def dot_nn(a, b):
    return jnp.dot(a, b, preferred_element_type=F32)


def dot_nt(a, b):
    return lax.dot_general(a, b, (((1,), (1,)), ((), ())), preferred_element_type=F32)


def dot_tn(a, b):
    return lax.dot_general(a, b, (((0,), (0,)), ((), ())), preferred_element_type=F32)


def pick_rows(col, k):
    shape = (col.shape[0], k)
    return jnp.where(lax.broadcasted_iota(I32, shape, 1) == col, 1.0, 0.0).astype(BF)


def put_rows(lane, first, m):
    shape = (m, lane.shape[1])
    here = lax.broadcasted_iota(I32, shape, 0) + first
    return jnp.where(here == lane, 1.0, 0.0).astype(BF)


def column(packed, g):
    lane = lax.broadcasted_iota(I32, packed.shape, 1)
    return jnp.sum(jnp.where(lane == g, packed, 0), axis=1, keepdims=True)


def sigmoid(v):
    return 1.0 / (1.0 + jnp.exp(-v))


def silu_pair(z):
    sig = sigmoid(z)
    return (z * sig).astype(BF), (sig * (1.0 + z * (1.0 - sig))).astype(BF)


def arrange_kernel(cap, uo_ref, ur_ref, io_ref, ir_ref, lab_ref, req_ref, lanes_ref, cols_ref):
    blocks = uo_ref.shape[0]
    owners = 16
    upto = jnp.where(
        lax.broadcasted_iota(I32, (128, 128), 0) <= lax.broadcasted_iota(I32, (128, 128), 1),
        1.0, 0.0,
    ).astype(BF)

    def ranks(owner):
        chosen = [
            jnp.where(
                lax.broadcasted_iota(I32, (owners, 128), 0) == owner[j : j + 1, :], 1.0, 0.0
            )
            for j in range(blocks)
        ]
        running = dot_nn(jnp.concatenate(chosen, axis=0).astype(BF), upto)
        before = jnp.zeros((owners, 1), F32)
        places = []
        for j in range(blocks):
            run = running[j * owners : (j + 1) * owners]
            places.append(
                jnp.sum(chosen[j] * (run + (before - 1.0)), axis=0, keepdims=True)
            )
            before = before + run[:, 127:128]
        return chosen, places

    def split(v):
        high = v >> 6
        return high.astype(F32), (v - (high << 6)).astype(F32)

    def spread(chosen, values):
        return jnp.concatenate(
            [c * v for c, v in zip(chosen, values)], axis=1
        ).astype(BF)

    def slots_of(places):
        sub = lax.broadcasted_iota(I32, (256, 128), 0)
        return jnp.concatenate(
            [jnp.where(sub == p.astype(I32), 1.0, 0.0) for p in places], axis=1
        ).astype(BF)

    uo, ur, io, ir, lab = (r[...] for r in (uo_ref, ur_ref, io_ref, ir_ref, lab_ref))
    u_chosen, u_places = ranks(uo)
    i_chosen, i_places = ranks(io)
    u_slots, i_slots = slots_of(u_places), slots_of(i_places)

    def rows(v):
        return [v[j : j + 1] for j in range(blocks)]

    ur_hi, ur_lo = split(ur)
    ir_hi, ir_lo = split(ir)
    item_slot = [
        io[j : j + 1] * cap + i_places[j].astype(I32) for j in range(blocks)
    ]
    is_hi, is_lo = split(jnp.concatenate(item_slot, axis=0))
    flag = (lab + 1).astype(F32)

    def wanted(chosen, slots, hi, lo):
        return dot_nt(spread(chosen, rows(hi)), slots) * 64.0 + dot_nt(
            spread(chosen, rows(lo)), slots
        )

    req = jnp.concatenate(
        [wanted(u_chosen, u_slots, ur_hi, ur_lo), wanted(i_chosen, i_slots, ir_hi, ir_lo)], axis=1
    ).astype(I32)
    for o in range(owners):
        req_ref[o] = req[o : o + 1]
    s_hi, s_lo = spread(u_chosen, rows(is_hi)), spread(u_chosen, rows(is_lo))
    s_flag = spread(u_chosen, rows(flag))
    lanes_ref[...] = (dot_nt(s_hi, u_slots) * 64.0 + dot_nt(s_lo, u_slots)).astype(I32)
    cols_ref[0] = (dot_nt(u_slots, s_hi) * 64.0 + dot_nt(u_slots, s_lo)).astype(I32)
    cols_ref[1] = dot_nt(u_slots, s_flag).astype(I32)


def fetch_kernel(asked_ref, ut_ref, it_ref, out_ref):
    peers, both, width = out_ref.shape
    cap = both // 2
    first = pl.program_id(0) * peers
    rows = [asked_ref[first + q] for q in range(peers)]
    for t, table in enumerate((ut_ref, it_ref)):
        lanes = jnp.concatenate([r[:, t * 256 : (t + 1) * 256] for r in rows + rows], axis=0)
        cols = jnp.transpose(lanes)
        col = jnp.concatenate([cols[:cap, q : q + 1] for q in range(peers)], axis=0)
        got = dot_nn(pick_rows(col, table.shape[0]), table[...]).astype(BF)
        out_ref[:, t * cap : (t + 1) * cap, :] = got.reshape(peers, cap, width)


def forward_kernel(
    icol_ref, um_ref, im_ref, w1u_ref, w1i_ref, w2_ref, w3_ref, wo_ref,
    im_out, a1_out, s1_out, a2_out, s2_out, a3_out, s3_out, deep_out,
):
    g = pl.program_id(0)
    m = um_ref.shape[0] * um_ref.shape[1]
    slots = im_ref.shape[0] * im_ref.shape[1]
    um = um_ref[...].reshape(m, D)
    sel = pick_rows(column(icol_ref[...], g), slots)
    im = dot_nn(sel, im_ref[...].reshape(slots, D)).astype(BF)
    im_out[...] = im
    z1 = dot_nn(um, w1u_ref[...]).astype(BF).astype(F32) + dot_nn(im, w1i_ref[...]).astype(
        BF
    ).astype(F32)
    a1, s1 = silu_pair(z1)
    a1_out[...], s1_out[...] = a1, s1
    a2, s2 = silu_pair(dot_nn(a1, w2_ref[...]))
    a2_out[...], s2_out[...] = a2, s2
    a3, s3 = silu_pair(dot_nn(a2, w3_ref[...]))
    a3_out[...], s3_out[...] = a3, s3
    deep = jnp.sum(a3.astype(F32) * wo_ref[:, D:], axis=1, keepdims=True)
    deep_out[...] = jnp.broadcast_to(deep, deep_out.shape)


def middle_kernel(
    icol_ref, fcol_ref, ilane_ref, ug_ref, ig_ref, deep_ref, wo_ref,
    out_ref, delta_out, go_out, gi_scr,
):
    step = pl.program_id(0)
    groups = pl.num_programs(0) // 2
    peers, cap, _ = ug_ref.shape
    m = peers * cap
    slots = ig_ref.shape[0] * cap

    @pl.when(step < groups)
    def _():
        ug = ug_ref[...].reshape(m, D).astype(F32)
        sel = pick_rows(column(icol_ref[...], step), slots)
        ig = dot_nn(sel, ig_ref[...].reshape(slots, D))
        wg = wo_ref[:, :D]
        prod = ug * ig
        logit = jnp.sum(prod * wg, axis=1, keepdims=True) + deep_ref[:, 0:1]
        flag = column(fcol_ref[...], step)
        delta = sigmoid(logit) - (flag - 1).astype(F32)
        delta = jnp.where(flag > 0, delta, 0.0)
        delta_out[...] = jnp.broadcast_to(delta, delta_out.shape)
        dw = delta * wg
        out_ref[...] = (dw * ig).astype(BF).reshape(peers, cap, D)
        gi_scr[pl.ds(pl.multiple_of(step * m, m), m), :] = (dw * ug).astype(BF)
        part = jnp.sum(delta * prod, axis=0, keepdims=True)

        @pl.when(step == 0)
        def _():
            go_out[...] = part

        @pl.when(step > 0)
        def _():
            go_out[...] += part

    @pl.when(step >= groups)
    def _():
        sel = put_rows(ilane_ref[...], (step - groups) * m, m)
        out_ref[...] = dot_nn(sel, gi_scr[...]).astype(BF).reshape(peers, cap, D)


def backward_kernel(
    me_ref, delta_ref, um_ref, im_ref, a1_ref, s1_ref, a2_ref, s2_ref, a3_ref, s3_ref,
    w2_ref, w3_ref, wo_ref, go_ref, d1_out, keep_out, give_out, gw_ref,
):
    step = pl.program_id(0)
    m = um_ref.shape[0] * um_ref.shape[1]
    um = um_ref[...].reshape(m, D)
    delta = delta_ref[:, 0:1]

    @pl.when(step == 0)
    def _():
        gw_ref[...] = jnp.zeros_like(gw_ref)
        gw_ref[WO : WO + 1, 0:D] = go_ref[...]

    d3 = (delta * wo_ref[:, D:] * s3_ref[...].astype(F32)).astype(BF)
    d2 = (dot_nt(d3, w3_ref[...]) * s2_ref[...].astype(F32)).astype(BF)
    d1 = (dot_nt(d2, w2_ref[...]) * s1_ref[...].astype(F32)).astype(BF)
    d1_out[...] = d1
    gw_ref[W1U:W1I, :] += dot_tn(um, d1)
    gw_ref[W1I:W2, :] += dot_tn(im_ref[...], d1)
    gw_ref[W2:W3, :] += dot_tn(a1_ref[...], d2)
    gw_ref[W3:WO, :] += dot_tn(a2_ref[...], d3)
    gw_ref[WO + 1 : WO + 2, :] += jnp.sum(
        delta * a3_ref[...].astype(F32), axis=0, keepdims=True
    )

    @pl.when(step == pl.num_programs(0) - 1)
    def _():
        y, core = me_ref[0] // 2, me_ref[0] % 2
        for half, out in ((core, keep_out), (1 - core, give_out)):
            at = 0
            for j in range(4):
                peer = (y + j) % 4 * 2 + half
                for first, count in PARTS:
                    start = pl.multiple_of(first + peer * count, 8)
                    out[at : at + count, :] = gw_ref[pl.ds(start, count), :].astype(BF)
                    at += count


def rows_kernel(ilane_ref, d1_ref, w1u_ref, w1i_ref, out_ref, mi_scr):
    step = pl.program_id(0)
    groups = pl.num_programs(0) // 2
    peers, cap, _ = out_ref.shape
    m = peers * cap

    @pl.when(step < groups)
    def _():
        d1 = d1_ref[...]
        out_ref[...] = dot_nt(d1, w1u_ref[...]).astype(BF).reshape(peers, cap, D)
        mi_scr[pl.ds(pl.multiple_of(step * m, m), m), :] = dot_nt(d1, w1i_ref[...]).astype(BF)

    @pl.when(step >= groups)
    def _():
        sel = put_rows(ilane_ref[...], (step - groups) * m, m)
        out_ref[...] = dot_nn(sel, mi_scr[...]).astype(BF).reshape(peers, cap, D)


def assemble_kernel(scale, me_ref, *refs):
    chunks, outs = refs[:8], refs[8:]
    y, core = me_ref[0] // 2, me_ref[0] % 2
    for k, chunk in enumerate(chunks):
        half = core if k < 4 else 1 - core
        peer = (y + 4 - k % 4) % 4 * 2 + half
        at = 0
        for (_, count), out in zip(PARTS, outs):
            rows = chunk[at : at + count, :].astype(F32) * scale
            out[pl.ds(pl.multiple_of(peer * count, 8), count), :] = rows
            at += count


def gather_add_kernel(lane_ref, terms_ref, *rest):
    user_out, item_out = rest[-2:]
    step = pl.program_id(0)
    steps = pl.num_programs(0) // 2
    m = user_out.shape[0]
    slots = terms_ref.shape[0] * terms_ref.shape[1]
    sel = put_rows(lane_ref[0], step % steps * m, m)
    got = dot_nn(sel, terms_ref[...].reshape(slots, D))

    @pl.when(step < steps)
    def _():
        user_out[...] = got

    @pl.when(step >= steps)
    def _():
        item_out[...] = got


def whole(shape):
    return pl.BlockSpec(shape, lambda i: (0,) * len(shape))


def body(
    user_table, item_table, user_owner, user_row, item_owner, item_row, labels,
    w1_user, w1_item, w2_weight, w3_weight, w_out,
):
    owners = lax.axis_size("emb")
    pairs = labels.shape[0]
    rows = user_table.shape[0]
    cap = 3 * pairs // (2 * owners)
    slots = owners * cap
    groups = 4
    peers = owners // groups
    m = peers * cap
    hid = w2_weight.shape[0]
    blocks = pairs // 128
    wo = w_out.reshape(1, -1)

    def call(kernel, grid, in_specs, out_specs, out_shape, scratch=(), aliases=None, flops=0, moved=0):
        return pl.pallas_call(
            kernel, grid=grid, in_specs=in_specs, out_specs=out_specs, out_shape=out_shape,
            scratch_shapes=scratch, input_output_aliases=aliases or {}, compiler_params=PARAMS,
            cost_estimate=pl.CostEstimate(flops=flops // 64, bytes_accessed=moved // 64, transcendentals=0),
        )

    def exchange(x):
        return lax.all_to_all(x, "emb", split_axis=0, concat_axis=0, tiled=True)

    req, lanes, cols = pl.pallas_call(
        functools.partial(arrange_kernel, cap),
        out_shape=(
            jax.ShapeDtypeStruct((owners, 1, 512), I32),
            jax.ShapeDtypeStruct((owners, 256), I32),
            jax.ShapeDtypeStruct((2, 256, owners), I32),
        ),
        compiler_params=PARAMS,
    )(*(a.reshape(blocks, 128) for a in (user_owner, user_row, item_owner, item_row, labels)))

    asked = exchange(req)
    wanted = asked.reshape(owners, 2, 256)[:, :, :cap]
    wlane = wanted.transpose(1, 0, 2).reshape(2, 1, slots)
    ilane = lanes[:, :cap].reshape(1, slots)
    side = cols[:, :cap, :].reshape(2, cap, groups, peers).transpose(0, 3, 1, 2)
    side = side.reshape(2, m, groups)
    icol, fcol = side[0], side[1]

    buffer = jax.ShapeDtypeStruct((owners, 2 * cap, D), BF)
    user_block = pl.BlockSpec((peers, cap, D), lambda i: (i, 0, 0))
    all_items = pl.BlockSpec((owners, cap, D), lambda i: (0, 1, 0))
    tile = pl.BlockSpec((m, hid), lambda i: (i, 0))
    narrow = pl.BlockSpec((m, D), lambda i: (i, 0))
    thin = pl.BlockSpec((m, 128), lambda i: (i, 0))
    weights = [whole((D, hid)), whole((D, hid)), whole((hid, hid)), whole((hid, hid))]
    wide = jax.ShapeDtypeStruct((slots, hid), BF)
    pick = 2 * slots * slots * D

    def fetch(half):
        table = pl.BlockSpec((rows, D), lambda i: (0, half))
        return call(
            fetch_kernel, (groups,), [whole((owners, 1, 512)), table, table],
            pl.BlockSpec((peers, 2 * cap, D), lambda i: (i, 0, 0)), buffer,
            flops=4 * slots * rows * D, moved=4 * slots * D + 4 * rows * D,
        )(asked, user_table, item_table)

    mlp_back = exchange(fetch(1))
    gmf_back = exchange(fetch(0))

    im, a1, s1, a2, s2, a3, s3, deep = call(
        forward_kernel, (groups,),
        [whole((m, groups)), user_block, all_items, *weights, whole((1, D + hid))],
        [narrow, tile, tile, tile, tile, tile, tile, thin],
        [jax.ShapeDtypeStruct((slots, D), BF)] + [wide] * 6 + [jax.ShapeDtypeStruct((slots, 128), F32)],
        flops=pick + 2 * slots * hid * (2 * D + 2 * hid), moved=16 * slots * hid,
    )(icol, mlp_back, mlp_back, w1_user, w1_item, w2_weight, w3_weight, wo)

    last = groups - 1
    gmf_out, delta, go = call(
        middle_kernel, (2 * groups,),
        [
            whole((m, groups)), whole((m, groups)), whole((1, slots)),
            pl.BlockSpec((peers, cap, D), lambda i: (jnp.minimum(i, last), 0, 0)), all_items,
            pl.BlockSpec((m, 128), lambda i: (jnp.minimum(i, last), 0)), whole((1, D + hid)),
        ],
        [
            pl.BlockSpec((peers, cap, D), lambda i: (i % groups, i // groups, 0)),
            pl.BlockSpec((m, 128), lambda i: (jnp.minimum(i, last), 0)), whole((1, D)),
        ],
        [buffer, jax.ShapeDtypeStruct((slots, 128), F32), jax.ShapeDtypeStruct((1, D), F32)],
        scratch=[pltpu.VMEM((slots, D), BF)], flops=2 * pick, moved=12 * slots * D,
    )(icol, fcol, ilane, gmf_back, gmf_back, deep, wo)

    gmf_terms = exchange(gmf_out)

    me = lax.axis_index("dp").astype(I32).reshape(1)
    n_dp = lax.axis_size("dp")
    scalar = pl.BlockSpec(memory_space=pltpu.SMEM)
    stack = jax.ShapeDtypeStruct((4 * CHUNK, hid), BF)
    fine = groups
    small_tile = pl.BlockSpec((slots // fine, hid), lambda i: (i, 0))
    d1, keep, give = call(
        backward_kernel, (fine,),
        [scalar, pl.BlockSpec((slots // fine, 128), lambda i: (i, 0)),
         pl.BlockSpec((owners // fine, cap, D), lambda i: (i, 0, 0)),
         pl.BlockSpec((slots // fine, D), lambda i: (i, 0)), *[small_tile] * 6,
         whole((hid, hid)), whole((hid, hid)), whole((1, D + hid)), whole((1, D))],
        [small_tile, whole((4 * CHUNK, hid)), whole((4 * CHUNK, hid))], [wide, stack, stack],
        scratch=[pltpu.VMEM((WEND, hid), F32)],
        flops=2 * slots * hid * (2 * D + 4 * hid), moved=16 * slots * hid,
    )(me, delta, mlp_back, im, a1, s1, a2, s2, a3, s3, w2_weight, w3_weight, wo, go)

    mlp_out = call(
        rows_kernel, (2 * groups,),
        [whole((1, slots)), pl.BlockSpec((m, hid), lambda i: (jnp.minimum(i, last), 0)),
         whole((D, hid)), whole((D, hid))],
        pl.BlockSpec((peers, cap, D), lambda i: (i % groups, i // groups, 0)), buffer,
        scratch=[pltpu.VMEM((slots, D), BF)], flops=pick + 4 * slots * hid * D,
        moved=4 * slots * hid,
    )(ilane, d1, w1_user, w1_item)

    def gather_add(terms, half, *into):
        steps = 2
        r = rows // steps
        grad = jax.ShapeDtypeStruct((rows, 2 * D), F32)
        return call(
            gather_add_kernel, (2 * steps,),
            [pl.BlockSpec((1, 1, slots), lambda i: (i // steps, 0, 0)),
             pl.BlockSpec((owners, cap, D), lambda i: (0, i // steps, 0))]
            + [pl.BlockSpec(memory_space=pl.ANY)] * len(into),
            [pl.BlockSpec((r, D), lambda i: (jnp.minimum(i, steps - 1), half)),
             pl.BlockSpec((r, D), lambda i: (jnp.maximum(i - steps, 0), half))],
            [grad, grad], aliases={2 + k: k for k in range(len(into))},
            flops=4 * rows * slots * D, moved=4 * slots * D + 8 * rows * D,
        )(wlane, terms, *into)

    def shift_dp(x, k):
        return lax.ppermute(x, "dp", [(s, (s + k) % n_dp) for s in range(n_dp)])

    def shift_emb(x, kx, kz):
        side = 4
        return lax.ppermute(
            x, "emb",
            [
                (a * side + b, (a + kx) % side * side + (b + kz) % side)
                for a in range(side) for b in range(side)
            ],
        )

    def ring_sum(v, step):
        v = lax.optimization_barrier(v.astype(BF))
        one, two, three = (step(v, k).astype(F32) for k in (1, 2, 3))
        return (v.astype(F32) + two) + (one + three)

    def swap_core(x):
        return lax.ppermute(x, "dp", [(s, s ^ 1) for s in range(n_dp)])

    got = swap_core(give)
    both = [
        keep[j * CHUNK : (j + 1) * CHUNK].astype(F32) + got[j * CHUNK : (j + 1) * CHUNK].astype(F32)
        for j in range(4)
    ]
    part = both[0]
    for j in range(1, 4):
        part = part + shift_dp(both[j].astype(BF), 2 * j).astype(F32)
    mlp_out, part = lax.optimization_barrier((mlp_out, part))

    def over_x(v, k):
        return shift_emb(v, k, 0)

    def over_z(v, k):
        return shift_emb(v, 0, k)

    top, low = part[:HALF], part[HALF:]
    top, low = ring_sum(top, over_x), ring_sum(low, over_z)
    top, low = ring_sum(top, over_z), ring_sum(low, over_x)
    mlp_out, top, low = lax.optimization_barrier((mlp_out, top, low))
    mlp_terms = exchange(mlp_out)
    part = jnp.concatenate([top, low]).astype(BF)
    user_grad, item_grad = gather_add(gmf_terms, 0)
    found = [part] + [shift_dp(part, 2 * j) for j in range(1, 4)]
    found = found + [swap_core(v) for v in found]
    gw1u, gw1i, gw2, gw3, gwo = pl.pallas_call(
        functools.partial(assemble_kernel, 1.0 / pairs),
        in_specs=[scalar] + [pl.BlockSpec(memory_space=pltpu.VMEM)] * n_dp,
        out_shape=[jax.ShapeDtypeStruct((count * n_dp, hid), F32) for _, count in PARTS],
        compiler_params=PARAMS,
    )(me, *found)

    grad_out = jnp.concatenate([gwo[0, :D], gwo[1]])
    mlp_terms, user_grad, item_grad, grad_out = lax.optimization_barrier(
        (mlp_terms, user_grad, item_grad, grad_out)
    )
    user_grad, item_grad = gather_add(mlp_terms, 1, user_grad, item_grad)
    return user_grad[None], item_grad[None], gw1u, gw1i, gw2, gw3, grad_out


def solution(mesh):
    return jax.shard_map(
        body,
        mesh=mesh,
        in_specs=(
            P("emb", None), P("emb", None), P(ROWS, None), P(ROWS), P(ROWS, None), P(ROWS), P(ROWS),
            P(), P(), P(), P(), P(),
        ),
        out_specs=(P("dp", "emb", None), P("dp", "emb", None), P(), P(), P(), P(), P()),
        check_vma=False,
    )
```

```python
import functools

import jax
import jax.numpy as jnp
from jax import lax
from jax.experimental import pallas as pl
from jax.experimental.pallas import tpu as pltpu
from jax.sharding import PartitionSpec as P

D = 256
BF, F32, I32 = jnp.bfloat16, jnp.float32, jnp.int32
ROWS = ("emb", "dp")


PARAMS = pltpu.CompilerParams(vmem_limit_bytes=63 << 20)


W1U, W1I, W2, W3, WO, WEND = 0, 256, 512, 1024, 1536, 1600
PARTS = ((W1U, 32), (W1I, 32), (W2, 64), (W3, 64), (WO, 8))
CHUNK, HALF = 200, 104


def dot_nn(a, b):
    return jnp.dot(a, b, preferred_element_type=F32)


def dot_nt(a, b):
    return lax.dot_general(a, b, (((1,), (1,)), ((), ())), preferred_element_type=F32)


def dot_tn(a, b):
    return lax.dot_general(a, b, (((0,), (0,)), ((), ())), preferred_element_type=F32)


def pick_rows(col, k):
    shape = (col.shape[0], k)
    return jnp.where(lax.broadcasted_iota(I32, shape, 1) == col, 1.0, 0.0).astype(BF)


def put_rows(lane, first, m):
    shape = (m, lane.shape[1])
    here = lax.broadcasted_iota(I32, shape, 0) + first
    return jnp.where(here == lane, 1.0, 0.0).astype(BF)


def column(packed, g):
    lane = lax.broadcasted_iota(I32, packed.shape, 1)
    return jnp.sum(jnp.where(lane == g, packed, 0), axis=1, keepdims=True)


def sigmoid(v):
    return 1.0 / (1.0 + jnp.exp(-v))


def silu_pair(z):
    sig = sigmoid(z)
    return (z * sig).astype(BF), (sig * (1.0 + z * (1.0 - sig))).astype(BF)


def arrange_kernel(cap, ask, uo_ref, ur_ref, io_ref, ir_ref, lab_ref, *outs):
    blocks = uo_ref.shape[0]
    owners = 16
    upto = jnp.where(
        lax.broadcasted_iota(I32, (128, 128), 0) <= lax.broadcasted_iota(I32, (128, 128), 1),
        1.0, 0.0,
    ).astype(BF)

    def ranks(owner):
        chosen = [
            jnp.where(
                lax.broadcasted_iota(I32, (owners, 128), 0) == owner[j : j + 1, :], 1.0, 0.0
            )
            for j in range(blocks)
        ]
        running = dot_nn(jnp.concatenate(chosen, axis=0).astype(BF), upto)
        before = jnp.zeros((owners, 1), F32)
        places = []
        for j in range(blocks):
            run = running[j * owners : (j + 1) * owners]
            places.append(
                jnp.sum(chosen[j] * (run + (before - 1.0)), axis=0, keepdims=True)
            )
            before = before + run[:, 127:128]
        return chosen, places

    def split(v):
        high = v >> 6
        return high.astype(F32), (v - (high << 6)).astype(F32)

    def spread(chosen, values):
        return jnp.concatenate(
            [c * v for c, v in zip(chosen, values)], axis=1
        ).astype(BF)

    def slots_of(places):
        sub = lax.broadcasted_iota(I32, (256, 128), 0)
        return jnp.concatenate(
            [jnp.where(sub == p.astype(I32), 1.0, 0.0) for p in places], axis=1
        ).astype(BF)

    uo, ur, io, ir, lab = (r[...] for r in (uo_ref, ur_ref, io_ref, ir_ref, lab_ref))
    u_chosen, u_places = ranks(uo)
    i_chosen, i_places = ranks(io)
    u_slots, i_slots = slots_of(u_places), slots_of(i_places)

    def rows(v):
        return [v[j : j + 1] for j in range(blocks)]

    ur_hi, ur_lo = split(ur)
    ir_hi, ir_lo = split(ir)
    item_slot = [
        io[j : j + 1] * cap + i_places[j].astype(I32) for j in range(blocks)
    ]
    is_hi, is_lo = split(jnp.concatenate(item_slot, axis=0))
    flag = (lab + 1).astype(F32)

    def wanted(chosen, slots, hi, lo):
        return dot_nt(spread(chosen, rows(hi)), slots) * 64.0 + dot_nt(
            spread(chosen, rows(lo)), slots
        )

    if ask:
        req = jnp.concatenate(
            [wanted(u_chosen, u_slots, ur_hi, ur_lo), wanted(i_chosen, i_slots, ir_hi, ir_lo)], axis=1
        ).astype(I32)
        for o in range(owners):
            outs[0][o] = req[o : o + 1]
        return
    lanes_ref, cols_ref = outs
    s_hi, s_lo = spread(u_chosen, rows(is_hi)), spread(u_chosen, rows(is_lo))
    s_flag = spread(u_chosen, rows(flag))
    lanes_ref[...] = (dot_nt(s_hi, u_slots) * 64.0 + dot_nt(s_lo, u_slots)).astype(I32)
    cols_ref[0] = (dot_nt(u_slots, s_hi) * 64.0 + dot_nt(u_slots, s_lo)).astype(I32)
    cols_ref[1] = dot_nt(u_slots, s_flag).astype(I32)


def fetch_kernel(asked_ref, ut_ref, it_ref, out_ref):
    peers, both, width = out_ref.shape
    cap = both // 2
    first = pl.program_id(0) * peers
    rows = [asked_ref[first + q] for q in range(peers)]
    for t, table in enumerate((ut_ref, it_ref)):
        lanes = jnp.concatenate([r[:, t * 256 : (t + 1) * 256] for r in rows + rows], axis=0)
        cols = jnp.transpose(lanes)
        col = jnp.concatenate([cols[:cap, q : q + 1] for q in range(peers)], axis=0)
        got = dot_nn(pick_rows(col, table.shape[0]), table[...]).astype(BF)
        out_ref[:, t * cap : (t + 1) * cap, :] = got.reshape(peers, cap, width)


def forward_kernel(
    icol_ref, um_ref, im_ref, w1u_ref, w1i_ref, w2_ref, w3_ref, wo_ref,
    im_out, a1_out, s1_out, a2_out, s2_out, a3_out, s3_out, deep_out,
):
    g = pl.program_id(0)
    m = um_ref.shape[0] * um_ref.shape[1]
    slots = im_ref.shape[0] * im_ref.shape[1]
    um = um_ref[...].reshape(m, D)
    sel = pick_rows(column(icol_ref[...], g), slots)
    im = dot_nn(sel, im_ref[...].reshape(slots, D)).astype(BF)
    im_out[...] = im
    z1 = dot_nn(um, w1u_ref[...]).astype(BF).astype(F32) + dot_nn(im, w1i_ref[...]).astype(
        BF
    ).astype(F32)
    a1, s1 = silu_pair(z1)
    a1_out[...], s1_out[...] = a1, s1
    a2, s2 = silu_pair(dot_nn(a1, w2_ref[...]))
    a2_out[...], s2_out[...] = a2, s2
    a3, s3 = silu_pair(dot_nn(a2, w3_ref[...]))
    a3_out[...], s3_out[...] = a3, s3
    deep = jnp.sum(a3.astype(F32) * wo_ref[:, D:], axis=1, keepdims=True)
    deep_out[...] = jnp.broadcast_to(deep, deep_out.shape)


def middle_kernel(
    icol_ref, fcol_ref, ilane_ref, ug_ref, ig_ref, deep_ref, wo_ref,
    out_ref, delta_out, go_out, gi_scr,
):
    step = pl.program_id(0)
    groups = pl.num_programs(0) // 2
    peers, cap, _ = ug_ref.shape
    m = peers * cap
    slots = ig_ref.shape[0] * cap

    @pl.when(step < groups)
    def _():
        ug = ug_ref[...].reshape(m, D).astype(F32)
        sel = pick_rows(column(icol_ref[...], step), slots)
        ig = dot_nn(sel, ig_ref[...].reshape(slots, D))
        wg = wo_ref[:, :D]
        prod = ug * ig
        logit = jnp.sum(prod * wg, axis=1, keepdims=True) + deep_ref[:, 0:1]
        flag = column(fcol_ref[...], step)
        delta = sigmoid(logit) - (flag - 1).astype(F32)
        delta = jnp.where(flag > 0, delta, 0.0)
        delta_out[...] = jnp.broadcast_to(delta, delta_out.shape)
        dw = delta * wg
        out_ref[...] = (dw * ig).astype(BF).reshape(peers, cap, D)
        gi_scr[pl.ds(pl.multiple_of(step * m, m), m), :] = (dw * ug).astype(BF)
        part = jnp.sum(delta * prod, axis=0, keepdims=True)

        @pl.when(step == 0)
        def _():
            go_out[...] = part

        @pl.when(step > 0)
        def _():
            go_out[...] += part

    @pl.when(step >= groups)
    def _():
        sel = put_rows(ilane_ref[...], (step - groups) * m, m)
        out_ref[...] = dot_nn(sel, gi_scr[...]).astype(BF).reshape(peers, cap, D)


def backward_kernel(
    me_ref, delta_ref, um_ref, im_ref, a1_ref, s1_ref, a2_ref, s2_ref, a3_ref, s3_ref,
    w2_ref, w3_ref, wo_ref, go_ref, d1_out, keep_out, give_out, gw_ref,
):
    step = pl.program_id(0)
    m = um_ref.shape[0] * um_ref.shape[1]
    um = um_ref[...].reshape(m, D)
    delta = delta_ref[:, 0:1]

    @pl.when(step == 0)
    def _():
        gw_ref[...] = jnp.zeros_like(gw_ref)
        gw_ref[WO : WO + 1, 0:D] = go_ref[...]

    d3 = (delta * wo_ref[:, D:] * s3_ref[...].astype(F32)).astype(BF)
    d2 = (dot_nt(d3, w3_ref[...]) * s2_ref[...].astype(F32)).astype(BF)
    d1 = (dot_nt(d2, w2_ref[...]) * s1_ref[...].astype(F32)).astype(BF)
    d1_out[...] = d1
    gw_ref[W1U:W1I, :] += dot_tn(um, d1)
    gw_ref[W1I:W2, :] += dot_tn(im_ref[...], d1)
    gw_ref[W2:W3, :] += dot_tn(a1_ref[...], d2)
    gw_ref[W3:WO, :] += dot_tn(a2_ref[...], d3)
    gw_ref[WO + 1 : WO + 2, :] += jnp.sum(
        delta * a3_ref[...].astype(F32), axis=0, keepdims=True
    )

    @pl.when(step == pl.num_programs(0) - 1)
    def _():
        y, core = me_ref[0] // 2, me_ref[0] % 2
        for half, out in ((core, keep_out), (1 - core, give_out)):
            at = 0
            for j in range(4):
                peer = (y + j) % 4 * 2 + half
                for first, count in PARTS:
                    start = pl.multiple_of(first + peer * count, 8)
                    out[at : at + count, :] = gw_ref[pl.ds(start, count), :].astype(BF)
                    at += count


def rows_kernel(ilane_ref, d1_ref, w1u_ref, w1i_ref, out_ref, mi_scr):
    step = pl.program_id(0)
    groups = pl.num_programs(0) // 2
    peers, cap, _ = out_ref.shape
    m = peers * cap

    @pl.when(step < groups)
    def _():
        d1 = d1_ref[...]
        out_ref[...] = dot_nt(d1, w1u_ref[...]).astype(BF).reshape(peers, cap, D)
        mi_scr[pl.ds(pl.multiple_of(step * m, m), m), :] = dot_nt(d1, w1i_ref[...]).astype(BF)

    @pl.when(step >= groups)
    def _():
        sel = put_rows(ilane_ref[...], (step - groups) * m, m)
        out_ref[...] = dot_nn(sel, mi_scr[...]).astype(BF).reshape(peers, cap, D)


def assemble_kernel(scale, me_ref, *refs):
    chunks, outs = refs[:8], refs[8:]
    y, core = me_ref[0] // 2, me_ref[0] % 2
    for k, chunk in enumerate(chunks):
        half = core if k < 4 else 1 - core
        peer = (y + 4 - k % 4) % 4 * 2 + half
        at = 0
        for (_, count), out in zip(PARTS, outs):
            rows = chunk[at : at + count, :].astype(F32) * scale
            out[pl.ds(pl.multiple_of(peer * count, 8), count), :] = rows
            at += count


def gather_add_kernel(lane_ref, terms_ref, *rest):
    user_out, item_out = rest[-2:]
    step = pl.program_id(0)
    steps = pl.num_programs(0) // 2
    m = user_out.shape[0]
    slots = terms_ref.shape[0] * terms_ref.shape[1]
    sel = put_rows(lane_ref[0], step % steps * m, m)
    got = dot_nn(sel, terms_ref[...].reshape(slots, D))

    @pl.when(step < steps)
    def _():
        user_out[...] = got

    @pl.when(step >= steps)
    def _():
        item_out[...] = got


def whole(shape):
    return pl.BlockSpec(shape, lambda i: (0,) * len(shape))


def body(
    user_table, item_table, user_owner, user_row, item_owner, item_row, labels,
    w1_user, w1_item, w2_weight, w3_weight, w_out,
):
    owners = lax.axis_size("emb")
    pairs = labels.shape[0]
    rows = user_table.shape[0]
    cap = 3 * pairs // (2 * owners)
    slots = owners * cap
    groups = 4
    peers = owners // groups
    m = peers * cap
    hid = w2_weight.shape[0]
    blocks = pairs // 128
    wo = w_out.reshape(1, -1)

    def call(kernel, grid, in_specs, out_specs, out_shape, scratch=(), aliases=None, flops=0, moved=0):
        return pl.pallas_call(
            kernel, grid=grid, in_specs=in_specs, out_specs=out_specs, out_shape=out_shape,
            scratch_shapes=scratch, input_output_aliases=aliases or {}, compiler_params=PARAMS,
            cost_estimate=pl.CostEstimate(flops=flops // 64, bytes_accessed=moved // 64, transcendentals=0),
        )

    def exchange(x):
        return lax.all_to_all(x, "emb", split_axis=0, concat_axis=0, tiled=True)

    lists = [a.reshape(blocks, 128) for a in (user_owner, user_row, item_owner, item_row, labels)]

    def arrange(ask, out_shape, given):
        return pl.pallas_call(
            functools.partial(arrange_kernel, cap, ask), out_shape=out_shape, compiler_params=PARAMS
        )(*given)

    req = arrange(True, jax.ShapeDtypeStruct((owners, 1, 512), I32), lists)
    asked = exchange(req)
    wanted = asked.reshape(owners, 2, 256)[:, :, :cap]
    wlane = wanted.transpose(1, 0, 2).reshape(2, 1, slots)
    buffer = jax.ShapeDtypeStruct((owners, 2 * cap, D), BF)
    user_block = pl.BlockSpec((peers, cap, D), lambda i: (i, 0, 0))
    all_items = pl.BlockSpec((owners, cap, D), lambda i: (0, 1, 0))
    tile = pl.BlockSpec((m, hid), lambda i: (i, 0))
    narrow = pl.BlockSpec((m, D), lambda i: (i, 0))
    thin = pl.BlockSpec((m, 128), lambda i: (i, 0))
    weights = [whole((D, hid)), whole((D, hid)), whole((hid, hid)), whole((hid, hid))]
    wide = jax.ShapeDtypeStruct((slots, hid), BF)
    pick = 2 * slots * slots * D

    def fetch(half):
        table = pl.BlockSpec((rows, D), lambda i: (0, half))
        return call(
            fetch_kernel, (groups,), [whole((owners, 1, 512)), table, table],
            pl.BlockSpec((peers, 2 * cap, D), lambda i: (i, 0, 0)), buffer,
            flops=4 * slots * rows * D, moved=4 * slots * D + 4 * rows * D,
        )(asked, user_table, item_table)

    mlp_rows = fetch(1)
    mlp_back = exchange(mlp_rows)
    *later, _ = lax.optimization_barrier((*lists, mlp_rows))
    lanes, cols = arrange(
        False,
        (jax.ShapeDtypeStruct((owners, 256), I32), jax.ShapeDtypeStruct((2, 256, owners), I32)),
        later,
    )
    ilane = lanes[:, :cap].reshape(1, slots)
    side = cols[:, :cap, :].reshape(2, cap, groups, peers).transpose(0, 3, 1, 2)
    side = side.reshape(2, m, groups)
    icol, fcol = side[0], side[1]
    gmf_rows, ilane, icol, fcol = lax.optimization_barrier((fetch(0), ilane, icol, fcol))
    gmf_back = exchange(gmf_rows)

    im, a1, s1, a2, s2, a3, s3, deep = call(
        forward_kernel, (groups,),
        [whole((m, groups)), user_block, all_items, *weights, whole((1, D + hid))],
        [narrow, tile, tile, tile, tile, tile, tile, thin],
        [jax.ShapeDtypeStruct((slots, D), BF)] + [wide] * 6 + [jax.ShapeDtypeStruct((slots, 128), F32)],
        flops=pick + 2 * slots * hid * (2 * D + 2 * hid), moved=16 * slots * hid,
    )(icol, mlp_back, mlp_back, w1_user, w1_item, w2_weight, w3_weight, wo)

    last = groups - 1
    gmf_out, delta, go = call(
        middle_kernel, (2 * groups,),
        [
            whole((m, groups)), whole((m, groups)), whole((1, slots)),
            pl.BlockSpec((peers, cap, D), lambda i: (jnp.minimum(i, last), 0, 0)), all_items,
            pl.BlockSpec((m, 128), lambda i: (jnp.minimum(i, last), 0)), whole((1, D + hid)),
        ],
        [
            pl.BlockSpec((peers, cap, D), lambda i: (i % groups, i // groups, 0)),
            pl.BlockSpec((m, 128), lambda i: (jnp.minimum(i, last), 0)), whole((1, D)),
        ],
        [buffer, jax.ShapeDtypeStruct((slots, 128), F32), jax.ShapeDtypeStruct((1, D), F32)],
        scratch=[pltpu.VMEM((slots, D), BF)], flops=2 * pick, moved=12 * slots * D,
    )(icol, fcol, ilane, gmf_back, gmf_back, deep, wo)

    gmf_terms = exchange(gmf_out)

    me = lax.axis_index("dp").astype(I32).reshape(1)
    n_dp = lax.axis_size("dp")
    scalar = pl.BlockSpec(memory_space=pltpu.SMEM)
    stack = jax.ShapeDtypeStruct((4 * CHUNK, hid), BF)
    fine = groups
    small_tile = pl.BlockSpec((slots // fine, hid), lambda i: (i, 0))
    d1, keep, give = call(
        backward_kernel, (fine,),
        [scalar, pl.BlockSpec((slots // fine, 128), lambda i: (i, 0)),
         pl.BlockSpec((owners // fine, cap, D), lambda i: (i, 0, 0)),
         pl.BlockSpec((slots // fine, D), lambda i: (i, 0)), *[small_tile] * 6,
         whole((hid, hid)), whole((hid, hid)), whole((1, D + hid)), whole((1, D))],
        [small_tile, whole((4 * CHUNK, hid)), whole((4 * CHUNK, hid))], [wide, stack, stack],
        scratch=[pltpu.VMEM((WEND, hid), F32)],
        flops=2 * slots * hid * (2 * D + 4 * hid), moved=16 * slots * hid,
    )(me, delta, mlp_back, im, a1, s1, a2, s2, a3, s3, w2_weight, w3_weight, wo, go)

    mlp_out = call(
        rows_kernel, (2 * groups,),
        [whole((1, slots)), pl.BlockSpec((m, hid), lambda i: (jnp.minimum(i, last), 0)),
         whole((D, hid)), whole((D, hid))],
        pl.BlockSpec((peers, cap, D), lambda i: (i % groups, i // groups, 0)), buffer,
        scratch=[pltpu.VMEM((slots, D), BF)], flops=pick + 4 * slots * hid * D,
        moved=4 * slots * hid,
    )(ilane, d1, w1_user, w1_item)

    def gather_add(terms, half, *into):
        steps = 2
        r = rows // steps
        grad = jax.ShapeDtypeStruct((rows, 2 * D), F32)
        return call(
            gather_add_kernel, (2 * steps,),
            [pl.BlockSpec((1, 1, slots), lambda i: (i // steps, 0, 0)),
             pl.BlockSpec((owners, cap, D), lambda i: (0, i // steps, 0))]
            + [pl.BlockSpec(memory_space=pl.ANY)] * len(into),
            [pl.BlockSpec((r, D), lambda i: (jnp.minimum(i, steps - 1), half)),
             pl.BlockSpec((r, D), lambda i: (jnp.maximum(i - steps, 0), half))],
            [grad, grad], aliases={2 + k: k for k in range(len(into))},
            flops=4 * rows * slots * D, moved=4 * slots * D + 8 * rows * D,
        )(wlane, terms, *into)

    def shift_dp(x, k):
        return lax.ppermute(x, "dp", [(s, (s + k) % n_dp) for s in range(n_dp)])

    def shift_emb(x, kx, kz):
        side = 4
        return lax.ppermute(
            x, "emb",
            [
                (a * side + b, (a + kx) % side * side + (b + kz) % side)
                for a in range(side) for b in range(side)
            ],
        )

    def ring_sum(v, step):
        v = lax.optimization_barrier(v.astype(BF))
        one, two, three = (step(v, k).astype(F32) for k in (1, 2, 3))
        return (v.astype(F32) + two) + (one + three)

    def swap_core(x):
        return lax.ppermute(x, "dp", [(s, s ^ 1) for s in range(n_dp)])

    got = swap_core(give)
    both = [
        keep[j * CHUNK : (j + 1) * CHUNK].astype(F32) + got[j * CHUNK : (j + 1) * CHUNK].astype(F32)
        for j in range(4)
    ]
    part = both[0]
    for j in range(1, 4):
        part = part + shift_dp(both[j].astype(BF), 2 * j).astype(F32)
    mlp_out, part = lax.optimization_barrier((mlp_out, part))

    def over_x(v, k):
        return shift_emb(v, k, 0)

    def over_z(v, k):
        return shift_emb(v, 0, k)

    top, low = part[:HALF], part[HALF:]
    top, low = ring_sum(top, over_x), ring_sum(low, over_z)
    top, low = ring_sum(top, over_z), ring_sum(low, over_x)
    mlp_out, top, low = lax.optimization_barrier((mlp_out, top, low))
    mlp_terms = exchange(mlp_out)
    part = jnp.concatenate([top, low]).astype(BF)
    user_grad, item_grad = gather_add(gmf_terms, 0)
    found = [part] + [shift_dp(part, 2 * j) for j in range(1, 4)]
    found = found + [swap_core(v) for v in found]
    gw1u, gw1i, gw2, gw3, gwo = pl.pallas_call(
        functools.partial(assemble_kernel, 1.0 / pairs),
        in_specs=[scalar] + [pl.BlockSpec(memory_space=pltpu.VMEM)] * n_dp,
        out_shape=[jax.ShapeDtypeStruct((count * n_dp, hid), F32) for _, count in PARTS],
        compiler_params=PARAMS,
    )(me, *found)

    grad_out = jnp.concatenate([gwo[0, :D], gwo[1]])
    mlp_terms, user_grad, item_grad, grad_out = lax.optimization_barrier(
        (mlp_terms, user_grad, item_grad, grad_out)
    )
    user_grad, item_grad = gather_add(mlp_terms, 1, user_grad, item_grad)
    return user_grad[None], item_grad[None], gw1u, gw1i, gw2, gw3, grad_out


def solution(mesh):
    return jax.shard_map(
        body,
        mesh=mesh,
        in_specs=(
            P("emb", None), P("emb", None), P(ROWS, None), P(ROWS), P(ROWS, None), P(ROWS), P(ROWS),
            P(), P(), P(), P(), P(),
        ),
        out_specs=(P("dp", "emb", None), P("dp", "emb", None), P(), P(), P(), P(), P()),
        check_vma=False,
    )
```
